32 devices in a mesh: grid: 4 (over z), basis: 8 (over y, x, core).
Axes of the slice: x: 2, y: 2, z: 4, core: 2. Of those that a mesh axis runs over, the one named last changes fastest.
Arguments:
- basis_values: bfloat16 [512, 256, 512], P(('grid', 'basis')), may hold values from -6 to 6
- weights: float32 [512, 256], P(('grid', 'basis')), may hold values from 0.1 to 1
- points: bfloat16 [512, 3, 256], P(('grid', 'basis')), may hold values from 0 to 1
- block_lists: int32 [512, 4], P(('grid', 'basis')), may hold values from 0 to 31, as said below
- counts: int32 [8, 4], P('basis', 'grid'), may hold values from 1 to 16, 32 in all within a row
- density: bfloat16 [4096, 4096], P('basis'), may hold values from -0.25 to 0.25
- centers: float32 [3, 4096], replicated, may hold values from 0 to 1
- block_centers: float32 [3, 32], replicated, may hold values from 0 to 1
- block_exponents: float32 [32], replicated, may hold values from 2 to 20
Outputs:
- exchange_matrix: float32 [4096, 4096], P('basis', 'grid')
The draws below stay inside these ranges and needn't reach their ends.
Inputs may be any that keep to these rules, and one draw needn't show every extreme that they name: `block_lists`: each row names 4 different blocks. The rows of all devices with the same basis index name together exactly 8 different blocks, consecutive ones counted on from 31 to 0, and the rows of each such device name all 8 of them; one of them is named by every row of those devices. The blocks of basis index 0 begin at block 31. Entry [b, g] counts the live batches of the device at grid index g and basis index b, which are its first ones. Each row sums to 32 and its largest entry is 16.
All inputs are finite; a program needn't handle non-finite values.
Results may differ from the reference program's by a relative error of at most 0.0018.
Values may be sent and summed in bfloat16 or wider, within the bound.
A program may use at most 128 MiB of HBM per device.

```python
import math
import jax
import jax.numpy as jnp
import numpy as np
from jax import lax

TB = 128
LB = 4
CL = 8
P_SIZE = 256
BAT_DEV = 16
L = 512
NBLK = 32
NB = 4096
NBAT = 512
N_GRID = 4
N_BASIS = 8


def draw_block_lists(key, part):
    device_total = N_GRID * N_BASIS
    row_total = BAT_DEV * device_total
    others = CL - 1
    picked_count = LB - 1
    cover_rows = (others + picked_count - 1) // picked_count
    start_keys = jax.random.split(jax.random.fold_in(key, 11), 6)
    first_block = jax.random.randint(start_keys[0], (N_BASIS,), 0, NBLK)
    first_block = first_block.at[0].set(NBLK - 1)
    core_place = jax.random.randint(start_keys[1], (N_BASIS,), 0, CL)
    shuffle_others = jax.vmap(lambda chosen: jax.random.permutation(chosen, others))(jax.random.split(start_keys[2], N_BASIS))
    row_orders = jax.vmap(lambda chosen: jax.random.permutation(chosen, BAT_DEV))(jax.random.split(start_keys[3], device_total))
    free_offset = jax.random.randint(start_keys[4], (row_total,), 0, others)
    rotation = jax.random.randint(start_keys[5], (row_total,), 0, LB)
    row_index = jnp.arange(row_total, dtype=jnp.int32)
    device_at = row_index // BAT_DEV
    basis_at = device_at % N_BASIS
    ranked = row_orders[device_at, row_index % BAT_DEV]
    offset_at = jnp.where(ranked < cover_rows, ranked * picked_count, free_offset)
    steps_along = jnp.arange(picked_count, dtype=jnp.int32)
    other_slot = shuffle_others[basis_at[:, None], (offset_at[:, None] + steps_along[None, :]) % others]
    core_here = core_place[basis_at][:, None]
    cluster_slot = other_slot + (other_slot >= core_here).astype(jnp.int32)
    listed_slot = jnp.concatenate([core_here, cluster_slot], axis=1)
    turned = (jnp.arange(LB, dtype=jnp.int32)[None, :] + rotation[:, None]) % LB
    listed_slot = jnp.take_along_axis(listed_slot, turned, axis=1)
    return ((first_block[basis_at][:, None] + listed_slot) % NBLK).astype(jnp.int32)


def levels(stream_key, extent, cuts, least, high):
    gain, own = 1.0, jax.random.fold_in(stream_key, 6)
    for dim, blocks in cuts:
        heights = jnp.exp(jax.random.uniform(jax.random.fold_in(own, dim), (blocks,), jnp.float32, least / len(cuts), high / len(cuts)))
        gain = gain * jnp.repeat(heights, extent[dim] // blocks).reshape([-1 if axis == dim else 1 for axis in range(len(extent))])
    return gain


def split_up(count, total, limit, slope):
    weights = [(1 << 20) // math.isqrt(rank ** slope) + 1 for rank in range(2, count + 1)]
    rest, holding = total - limit - (count - 1), [1] * (count - 1)
    while rest > 0:
        candidates = [i for i in range(count - 1) if holding[i] < limit]
        whole, left = sum([weights[i] for i in candidates]), rest
        for i in candidates:
            extra = min(limit - holding[i], max(1, left * weights[i] // whole), rest)
            holding[i] = holding[i] + extra
            rest = rest - extra
    return np.array([limit] + holding)


def uneven(key, amount, total, most, skew):
    if amount == 2:
        one = jax.random.randint(key, (), max(1, total - most), min(most, total - 1) + 1)
        return jnp.stack([one, total - one])
    tallies = jnp.asarray(split_up(amount, total, most, skew), jnp.int32)
    couples = (amount - 1) // 2
    source_of, receiver = tallies[1:1 + 2 * couples:2], tallies[2:2 + 2 * couples:2]
    slack = jnp.minimum(source_of - 1, most - receiver)
    moved = jax.random.randint(jax.random.fold_in(key, 1), (couples,), 0, 1 << 20) % (slack + 1)
    tallies = tallies.at[1:1 + 2 * couples:2].set(source_of - moved).at[2:2 + 2 * couples:2].set(receiver + moved)
    return tallies[jax.random.permutation(jax.random.fold_in(key, 2), amount)]


def normal_values(key, dims, width, limit, cuts=(), kind=jnp.bfloat16):
    result = jax.random.normal(key, dims, jnp.float32) * width
    if len(cuts) > 0:
        result = levels(key, dims, cuts, -0.22, 0.18) * result
    return jnp.clip(result, min=-limit, max=limit).astype(kind)


def setup_inputs(seed: int = 0) -> dict:
    seeds = jax.random.split(jax.random.key(seed), 10)
    return {
        "basis_values": normal_values(seeds[0], (NBAT, P_SIZE, L), 1.0, 6.0, ((0, 32),)),
        "weights": jnp.clip(jnp.exp(math.log(1.0) - 2.3025851 * jax.random.uniform(seeds[1], (NBAT, P_SIZE), jnp.float32) ** levels(seeds[1], (NBAT, P_SIZE), ((0, 32),), -0.2, 0.2)), 0.1, 1.0),
        "points": jnp.clip(1.0 * jax.random.uniform(seeds[2], (NBAT, 3, P_SIZE), jnp.float32) ** levels(seeds[2], (NBAT, 3, P_SIZE), ((0, 32),), -0.2, 0.2), 0.0, 1.0).astype(jnp.bfloat16),
        "block_lists": draw_block_lists(jax.random.fold_in(seeds[9], 71), 0),
        "counts": jax.vmap(lambda own: uneven(own, N_GRID, N_GRID * BAT_DEV // 2, BAT_DEV, 2))(jax.random.split(seeds[4], N_BASIS)).reshape((N_BASIS, N_GRID)).astype(jnp.int32),
        "density": normal_values(seeds[5], (NB, NB), L ** -0.5, 0.25, ((0, 8),)),
        "centers": jnp.clip(jax.random.uniform(seeds[6], (3, NB), jnp.float32, 0.0, 1.0), 0.0, 1.0),
        "block_centers": jnp.clip(jax.random.uniform(seeds[7], (3, NBLK), jnp.float32, 0.0, 1.0), 0.0, 1.0),
        "block_exponents": jnp.clip(jnp.exp(jax.random.uniform(seeds[8], (NBLK,), jnp.float32, math.log(2.0), math.log(20.0))), 2.0, 20.0),
    }


def boys_single(points_f, blocks, block_centers, block_exponents):
    centre = block_centers[:, blocks]
    middle = 0.5 * (centre[:, :, None] + centre[:, None, :])
    exponents = block_exponents[blocks]
    rate_pair = 0.5 * (exponents[:, None] + exponents[None, :])
    offset = points_f[:, None, None, :] - middle[:, :, :, None]
    distance = lax.optimization_barrier(jnp.sum(offset * offset, axis=0))
    tau_value = rate_pair[:, :, None] * distance + 0.05
    root_value = jnp.sqrt(tau_value)
    return 0.5 * math.sqrt(math.pi) * lax.erf(root_value) / root_value

def coupling_single(blocks, centers):
    functions = (blocks[:, None] * TB + jnp.arange(TB, dtype=jnp.int32)[None, :]).reshape(L)
    where_at = centers[:, functions]
    spread = where_at[:, :, None] - where_at[:, None, :]
    distance = lax.optimization_barrier(jnp.sum(spread * spread, axis=0))
    sharpness = float(NB) ** (2.0 / 3.0)
    return jnp.exp(-sharpness * distance).astype(jnp.bfloat16)

def reference(basis_values, weights, points, block_lists, counts, density, centers, block_centers, block_exponents):
    density_tiles = density.reshape(NBLK, TB, NBLK, TB)

    def one_batch(accumulated, index):
        blocks = block_lists[index]
        grid_at = index // (N_BASIS * BAT_DEV)
        basis_at = index // BAT_DEV % N_BASIS
        within = index % BAT_DEV
        is_live = within < counts[basis_at, grid_at]
        dens_list = density_tiles[blocks[:, None], :, blocks[None, :], :]
        dens_list = dens_list.transpose(0, 2, 1, 3).reshape(L, L)
        values = basis_values[index]
        mapped = jnp.dot(values, dens_list.T, preferred_element_type=jnp.float32).astype(jnp.bfloat16)
        coupled = coupling_single(blocks, centers).reshape(LB, TB, LB, TB)
        partial_rows = jnp.einsum('puj,tiuj->ptui', mapped.reshape(P_SIZE, LB, TB).astype(jnp.float32), coupled.astype(jnp.float32), precision=lax.Precision.HIGHEST)
        factor = boys_single(points[index].astype(jnp.float32), blocks, block_centers, block_exponents)
        boys_weight = factor.transpose(2, 0, 1)[:, :, :, None]
        potential = lax.optimization_barrier(jnp.sum(partial_rows * boys_weight, axis=2)).astype(jnp.bfloat16).reshape(P_SIZE, L)
        scaled = jnp.where(is_live, weights[index], 0.0) / P_SIZE
        weighted = (values * scaled[:, None]).astype(jnp.bfloat16)
        batch_tile = jnp.dot(weighted.T, potential, preferred_element_type=jnp.float32)
        update = batch_tile.reshape(LB, TB, LB, TB).transpose(0, 2, 1, 3)
        accumulated = accumulated.at[blocks[:, None], :, blocks[None, :], :].add(update)
        return (accumulated, None)
    start_value = jnp.zeros((NBLK, TB, NBLK, TB), jnp.float32)
    accumulated, unused = lax.scan(one_batch, start_value, jnp.arange(NBAT, dtype=jnp.int32))
    return accumulated.reshape(NB, NB)
```

```python
import functools
import math

import jax
import jax.numpy as jnp
import numpy as np
from jax import lax
from jax.experimental import pallas as pl
from jax.experimental.pallas import tpu as pltpu
from jax.sharding import PartitionSpec as P

TB = 128
CL = 8


def boys_table(points_f, blocks, block_centers, block_exponents):
    centre = block_centers[:, blocks]
    middle = 0.5 * (centre[:, :, :, None] + centre[:, :, None, :])
    exponents = block_exponents[blocks]
    rate_pair = 0.5 * (exponents[:, :, None] + exponents[:, None, :])
    offset = points_f.transpose(1, 0, 2)[:, :, None, None, :] - middle[:, :, :, :, None]
    distance = jnp.sum(offset * offset, axis=0)
    tau_value = rate_pair[:, :, :, None] * distance + 0.05
    root_value = jnp.sqrt(tau_value)
    return 0.5 * math.sqrt(math.pi) * lax.erf(root_value) / root_value


def first_block_of(block_lists, block_count):
    present = jnp.any(
        block_lists.reshape(-1)[:, None] == jnp.arange(block_count, dtype=jnp.int32)[None, :],
        axis=0,
    )
    begins = present & jnp.logical_not(jnp.roll(present, 1))
    return jnp.sum(jnp.where(begins, jnp.arange(block_count, dtype=jnp.int32), 0))


def block_with_residue(first, residue, block_count):
    return (first + (residue - first) % CL) % block_count


def region_coupling(members, centers):
    functions = (members[:, None] * TB + jnp.arange(TB, dtype=jnp.int32)[None, :]).reshape(CL * TB)
    where_at = centers[:, functions].reshape(3, CL, TB)
    spread = where_at[:, :, None, :, None] - where_at[:, None, :, None, :]
    distance = jnp.sum(spread * spread, axis=0)
    sharpness = float(centers.shape[1]) ** (2.0 / 3.0)
    return jnp.exp(-sharpness * distance).astype(jnp.bfloat16)


def pack_kernel(column_ref, dens_ref, out_ref):
    out_ref[0, :, 0] = dens_ref[...].reshape(out_ref.shape[1], TB, TB)


def pack_density(columns, density, owned_blocks):
    targets, per = columns.shape
    return pl.pallas_call(
        pack_kernel,
        grid_spec=pltpu.PrefetchScalarGridSpec(
            num_scalar_prefetch=1,
            grid=(targets, per),
            in_specs=[pl.BlockSpec((owned_blocks * TB, TB), lambda t, c, col: (0, col[t, c]))],
            out_specs=pl.BlockSpec(
                (1, owned_blocks, 1, TB, TB), lambda t, c, col: (t, 0, c, 0, 0)
            ),
        ),
        out_shape=jax.ShapeDtypeStruct((targets, owned_blocks, per, TB, TB), jnp.bfloat16),
        name="pack_density",
    )(columns, density)


def batch_kernel(
    per, place_ref, count_ref, values_ref, weighted_ref, boys_ref, dens_ref, coup_ref, out_ref, acc
):
    n = pl.program_id(0)
    lists = place_ref.shape[1]

    @pl.when(n == 0)
    def _():
        acc[...] = jnp.zeros_like(acc)

    @pl.when(n < count_ref[0])
    def _():
        at = [place_ref[n, t] for t in range(lists)]
        dens = jnp.concatenate(
            [
                jnp.concatenate([dens_ref[c // per, r, c % per] for c in at], axis=1)
                for r in at
            ],
            axis=0,
        )
        mapped = lax.dot_general(
            dens, values_ref[0], (((1,), (1,)), ((), ())), preferred_element_type=jnp.float32
        ).astype(jnp.bfloat16)
        total = None
        for u in range(lists):
            coup = jnp.concatenate([coup_ref[r, at[u]] for r in at], axis=0)
            part = jnp.dot(
                coup, mapped[u * TB : (u + 1) * TB], preferred_element_type=jnp.float32
            )
            part = jnp.concatenate(
                [
                    part[t * TB : (t + 1) * TB]
                    * boys_ref[0, t * lists + u : t * lists + u + 1, :]
                    for t in range(lists)
                ],
                axis=0,
            )
            total = part if total is None else total + part
        tile = jnp.dot(
            total.astype(jnp.bfloat16), weighted_ref[0], preferred_element_type=jnp.float32
        )
        for c in range(lists):
            for r in range(lists):
                acc[at[c], at[r]] += tile[c * TB : (c + 1) * TB, r * TB : (r + 1) * TB]

    @pl.when(n == pl.num_programs(0) - 1)
    def _():
        def put(index, carry):
            c = index // CL
            r = index % CL
            out_ref[c // per, r, c % per] = acc[c, r].T.astype(out_ref.dtype)
            return carry

        lax.fori_loop(0, CL * CL, put, 0)


def region_exchange(places, count, values, weighted, boys, dens, coup, grid_size):
    batches, points, listed = values.shape
    per = CL // grid_size
    lists = places.shape[1]
    whole = lambda *shape: pl.BlockSpec(shape, lambda n, *_: (0,) * len(shape))
    return pl.pallas_call(
        functools.partial(batch_kernel, per),
        grid_spec=pltpu.PrefetchScalarGridSpec(
            num_scalar_prefetch=2,
            grid=(batches,),
            in_specs=[
                pl.BlockSpec((1, points, listed), lambda n, *_: (n, 0, 0)),
                pl.BlockSpec((1, points, listed), lambda n, *_: (n, 0, 0)),
                pl.BlockSpec((1, lists * lists, points), lambda n, *_: (n, 0, 0)),
                whole(grid_size, CL, per, TB, TB),
                whole(CL, CL, TB, TB),
            ],
            out_specs=whole(grid_size, CL, per, TB, TB),
            scratch_shapes=[pltpu.VMEM((CL, CL, TB, TB), jnp.float32)],
        ),
        out_shape=jax.ShapeDtypeStruct((grid_size, CL, per, TB, TB), jnp.bfloat16),
        compiler_params=pltpu.CompilerParams(vmem_limit_bytes=48 * 1024 * 1024),
        name="region_exchange",
    )(places, count, values, weighted, boys, dens, coup)


def body(
    basis_values,
    weights,
    points,
    block_lists,
    counts,
    density,
    centers,
    block_centers,
    block_exponents,
):
    basis_size = lax.axis_size("basis")
    grid_size = lax.axis_size("grid")
    me_basis = lax.axis_index("basis")
    me_grid = lax.axis_index("grid")
    block_count = block_exponents.shape[0]
    owned_blocks = block_count // basis_size
    turns = block_count // CL
    per = CL // grid_size
    batches, point_total = weights.shape
    lists = block_lists.shape[1]

    first = first_block_of(block_lists, block_count)
    firsts = lax.all_to_all(
        jnp.broadcast_to(first, (basis_size, 1)), "basis", split_axis=0, concat_axis=0, tiled=True
    )[:, 0]
    my_residues = me_grid * per + jnp.arange(per, dtype=jnp.int32)
    columns = block_with_residue(firsts[:, None], my_residues[None, :], block_count)

    packed = pack_density(columns, density, owned_blocks)
    tiles_in = lax.all_to_all(packed, "basis", split_axis=0, concat_axis=0, tiled=True)
    members = block_with_residue(first, jnp.arange(CL, dtype=jnp.int32), block_count)
    turn_of = members // CL
    chosen = (turn_of[None, :] == jnp.arange(turns, dtype=jnp.int32)[:, None])
    by_turn = tiles_in.reshape(turns, CL, per, TB, TB)
    mine = by_turn[0]
    for turn in range(1, turns):
        mine = jnp.where(chosen[turn][:, None, None, None], by_turn[turn], mine)
    dens = lax.all_to_all(
        jnp.broadcast_to(mine[None], (grid_size,) + mine.shape),
        "grid",
        split_axis=0,
        concat_axis=0,
        tiled=True,
    )

    coup = region_coupling(members, centers)
    boys = boys_table(
        points.astype(jnp.float32), block_lists, block_centers, block_exponents
    ).reshape(batches, lists * lists, point_total)
    live_count = counts[0, 0]
    is_live = jnp.arange(batches, dtype=jnp.int32) < live_count
    scaled = jnp.where(is_live[:, None], weights, 0.0) / point_total
    weighted = (basis_values * scaled[:, :, None]).astype(jnp.bfloat16)

    partial_sums = region_exchange(
        block_lists % CL, counts.reshape(1), basis_values, weighted, boys, dens, coup, grid_size
    )
    shares = lax.all_to_all(partial_sums, "grid", split_axis=0, concat_axis=0, tiled=True)
    segment = jnp.sum(shares.astype(jnp.float32), axis=0)

    outgoing = jnp.broadcast_to(segment[None], (turns,) + segment.shape).reshape(
        basis_size, owned_blocks, per, TB, TB
    )
    incoming = lax.all_to_all(outgoing, "basis", split_axis=0, concat_axis=0, tiled=True)
    my_blocks = me_basis * owned_blocks + jnp.arange(owned_blocks, dtype=jnp.int32)
    inside = (my_blocks[None, :] - firsts[:, None]) % block_count < CL
    takes = (
        inside[:, None, :, None]
        & (columns[:, None, None, :] // CL == jnp.arange(turns, dtype=jnp.int32)[None, :, None, None])
    )
    held = jnp.sum(
        jnp.where(takes[..., None, None], incoming[:, None], 0.0), axis=0
    )

    per_owner = block_count // grid_size
    if per_owner == CL:
        got = lax.all_to_all(held, "grid", split_axis=0, concat_axis=0, tiled=True)
        return got.transpose(1, 3, 0, 2, 4).reshape(owned_blocks * TB, per_owner * TB)
    held_blocks = np.array(
        [[q * CL + j * per + c for q in range(turns) for c in range(per)] for j in range(grid_size)]
    )
    room = max(
        int(np.sum(held_blocks[j] // per_owner == k))
        for j in range(grid_size)
        for k in range(grid_size)
    )
    send = np.zeros((grid_size, grid_size, room), np.int32)
    source = np.zeros((grid_size, per_owner), np.int32)
    for j in range(grid_size):
        filled = [0] * grid_size
        for at, block in enumerate(held_blocks[j]):
            k = int(block) // per_owner
            send[j, k, filled[k]] = at
            source[k, int(block) % per_owner] = j * room + filled[k]
            filled[k] += 1
    flat = held.transpose(0, 2, 1, 3, 4).reshape(turns * per, owned_blocks, TB, TB)
    going = flat[jnp.asarray(send)[me_grid].reshape(-1)].reshape(
        grid_size, room, owned_blocks, TB, TB
    )
    got = lax.all_to_all(going, "grid", split_axis=0, concat_axis=0, tiled=True)
    picked = got.reshape(grid_size * room, owned_blocks, TB, TB)[jnp.asarray(source)[me_grid]]
    return picked.transpose(1, 2, 0, 3).reshape(owned_blocks * TB, per_owner * TB)


def solution(mesh):
    placed = (
        P(("grid", "basis"), None, None),
        P(("grid", "basis"), None),
        P(("grid", "basis"), None, None),
        P(("grid", "basis"), None),
        P("basis", "grid"),
        P("basis", None),
        P(),
        P(),
        P(),
    )
    return jax.shard_map(
        body, mesh=mesh, in_specs=placed, out_specs=P("basis", "grid"), check_vma=False
    )
```

```python
import functools
import math

import jax
import jax.numpy as jnp
from jax import lax
from jax.experimental import pallas as pl
from jax.experimental.pallas import tpu as pltpu
from jax.sharding import PartitionSpec as P

TB = 128
CL = 8


def boys_table(points_f, blocks, block_centers, block_exponents):
    centre = block_centers[:, blocks]
    middle = 0.5 * (centre[:, :, :, None] + centre[:, :, None, :])
    exponents = block_exponents[blocks]
    rate_pair = 0.5 * (exponents[:, :, None] + exponents[:, None, :])
    offset = points_f.transpose(1, 0, 2)[:, :, None, None, :] - middle[:, :, :, :, None]
    distance = jnp.sum(offset * offset, axis=0)
    tau_value = rate_pair[:, :, :, None] * distance + 0.05
    root_value = jnp.sqrt(tau_value)
    return 0.5 * math.sqrt(math.pi) * lax.erf(root_value) / root_value


def first_block_of(block_lists, block_count):
    present = jnp.any(
        block_lists.reshape(-1)[:, None] == jnp.arange(block_count, dtype=jnp.int32)[None, :],
        axis=0,
    )
    begins = present & jnp.logical_not(jnp.roll(present, 1))
    return jnp.sum(jnp.where(begins, jnp.arange(block_count, dtype=jnp.int32), 0))


def block_with_residue(first, residue, block_count):
    return (first + (residue - first) % CL) % block_count


def region_coupling(members, centers):
    functions = (members[:, None] * TB + jnp.arange(TB, dtype=jnp.int32)[None, :]).reshape(CL * TB)
    where_at = centers[:, functions].reshape(3, CL, TB)
    spread = where_at[:, :, None, :, None] - where_at[:, None, :, None, :]
    distance = jnp.sum(spread * spread, axis=0)
    sharpness = float(centers.shape[1]) ** (2.0 / 3.0)
    return jnp.exp(-sharpness * distance).astype(jnp.bfloat16)


def pack_kernel(column_ref, dens_ref, out_ref):
    out_ref[0, :, 0] = dens_ref[...].reshape(out_ref.shape[1], TB, TB)


def pack_density(columns, density, owned_blocks):
    targets, per = columns.shape
    return pl.pallas_call(
        pack_kernel,
        grid_spec=pltpu.PrefetchScalarGridSpec(
            num_scalar_prefetch=1,
            grid=(targets, per),
            in_specs=[pl.BlockSpec((owned_blocks * TB, TB), lambda t, c, col: (0, col[t, c]))],
            out_specs=pl.BlockSpec(
                (1, owned_blocks, 1, TB, TB), lambda t, c, col: (t, 0, c, 0, 0)
            ),
        ),
        out_shape=jax.ShapeDtypeStruct((targets, owned_blocks, per, TB, TB), jnp.bfloat16),
        name="pack_density",
    )(columns, density)


def encode(tile):
    top = jnp.maximum(jnp.max(jnp.abs(tile), axis=0, keepdims=True), 1e-30)
    steps = jnp.round(tile * (32767.0 / top))
    return steps.astype(jnp.int32).astype(jnp.int16), top * (1.0 / 32767.0)


def decode(coded, scale):
    return coded.astype(jnp.int32).astype(jnp.float32) * scale


def batch_kernel(
    per, place_ref, count_ref, values_ref, weighted_ref, boys_ref, dens_ref, coup_ref, out_ref, scale_ref, acc
):
    n = pl.program_id(0)
    lists = place_ref.shape[1]

    @pl.when(n == 0)
    def _():
        acc[...] = jnp.zeros_like(acc)

    @pl.when(n < count_ref[0])
    def _():
        at = [place_ref[n, t] for t in range(lists)]
        dens = jnp.concatenate(
            [
                jnp.concatenate([dens_ref[c // per, r, c % per] for c in at], axis=1)
                for r in at
            ],
            axis=0,
        )
        mapped = lax.dot_general(
            dens, values_ref[0], (((1,), (1,)), ((), ())), preferred_element_type=jnp.float32
        ).astype(jnp.bfloat16)
        total = None
        for u in range(lists):
            coup = jnp.concatenate([coup_ref[r, at[u]] for r in at], axis=0)
            part = jnp.dot(
                coup, mapped[u * TB : (u + 1) * TB], preferred_element_type=jnp.float32
            )
            part = jnp.concatenate(
                [
                    part[t * TB : (t + 1) * TB]
                    * boys_ref[0, t * lists + u : t * lists + u + 1, :]
                    for t in range(lists)
                ],
                axis=0,
            )
            total = part if total is None else total + part
        tile = jnp.dot(
            total.astype(jnp.bfloat16), weighted_ref[0], preferred_element_type=jnp.float32
        )
        for c in range(lists):
            for r in range(lists):
                acc[at[c], at[r]] += tile[c * TB : (c + 1) * TB, r * TB : (r + 1) * TB]

    @pl.when(n == pl.num_programs(0) - 1)
    def _():
        def put(index, carry):
            c = index // CL
            r = index % CL
            coded, scale = encode(acc[c, r].T)
            out_ref[c // per, c % per, r] = coded
            scale_ref[c // per, c % per, pl.ds(r, 1), :] = scale
            return carry

        lax.fori_loop(0, CL * CL, put, 0)


def region_exchange(places, count, values, weighted, boys, dens, coup, grid_size):
    batches, points, listed = values.shape
    per = CL // grid_size
    lists = places.shape[1]
    whole = lambda *shape: pl.BlockSpec(shape, lambda n, *_: (0,) * len(shape))
    return pl.pallas_call(
        functools.partial(batch_kernel, per),
        grid_spec=pltpu.PrefetchScalarGridSpec(
            num_scalar_prefetch=2,
            grid=(batches,),
            in_specs=[
                pl.BlockSpec((1, points, listed), lambda n, *_: (n, 0, 0)),
                pl.BlockSpec((1, points, listed), lambda n, *_: (n, 0, 0)),
                pl.BlockSpec((1, lists * lists, points), lambda n, *_: (n, 0, 0)),
                whole(grid_size, CL, per, TB, TB),
                whole(CL, CL, TB, TB),
            ],
            out_specs=[
                whole(grid_size, per, CL, TB, TB),
                whole(grid_size, per, CL, TB),
            ],
            scratch_shapes=[pltpu.VMEM((CL, CL, TB, TB), jnp.float32)],
        ),
        out_shape=[
            jax.ShapeDtypeStruct((grid_size, per, CL, TB, TB), jnp.int16),
            jax.ShapeDtypeStruct((grid_size, per, CL, TB), jnp.float32),
        ],
        compiler_params=pltpu.CompilerParams(vmem_limit_bytes=48 * 1024 * 1024),
        name="region_exchange",
    )(places, count, values, weighted, boys, dens, coup)


def collect_kernel(
    grid_size,
    basis_size,
    owned,
    turns,
    kq,
    ks,
    takes,
    out,
    zq,
    zs,
    sq,
    ss,
    xq,
    xs,
    hq,
    hs,
    wq,
    ws,
    z_send,
    z_recv,
    x_send,
    x_recv,
    w_send,
    w_recv,
):
    per = CL // grid_size
    members = CL // owned
    per_owner = turns * per
    me_grid = lax.axis_index("grid")
    me_basis = lax.axis_index("basis")
    mine = lax.rem(me_basis, members)

    barrier = pltpu.get_barrier_semaphore()
    for d in range(1, grid_size):
        pl.semaphore_signal(
            barrier,
            inc=1,
            device_id=(lax.rem(me_grid + d, grid_size), me_basis),
            device_id_type=pl.DeviceIdType.MESH,
        )
    for d in range(1, basis_size):
        pl.semaphore_signal(
            barrier,
            inc=1,
            device_id=(me_grid, lax.rem(me_basis + d, basis_size)),
            device_id_type=pl.DeviceIdType.MESH,
        )
    pl.semaphore_wait(barrier, grid_size + basis_size - 2)

    def pair(sources, targets, sends, recvs, device):
        return [
            pltpu.make_async_remote_copy(
                src_ref=sources[which],
                dst_ref=targets[which],
                send_sem=sends.at[which],
                recv_sem=recvs.at[which],
                device_id=device,
                device_id_type=pl.DeviceIdType.MESH,
            )
            for which in range(2)
        ]

    def z_copy(cc, d):
        to = lax.rem(me_grid + d, grid_size)
        return pair(
            (kq.at[to, cc], ks.at[to, cc]),
            (zq.at[d - 1, cc], zs.at[d - 1, cc]),
            z_send.at[d - 1, cc],
            z_recv.at[d - 1, cc],
            (to, me_basis),
        )

    def x_copy(cc, d):
        to = lax.rem(me_basis + d, basis_size)
        its = lax.rem(to, members)
        return pair(
            (sq.at[cc, its], ss.at[cc, its]),
            (xq.at[d - 1, cc], xs.at[d - 1, cc]),
            x_send.at[d - 1, cc],
            x_recv.at[d - 1, cc],
            (me_grid, to),
        )

    def w_place(q):
        at = CL * q + me_grid * per
        return at // per_owner, lax.rem(at, per_owner) // per

    def w_copy(cc, q):
        to, slot = w_place(q)
        return pair(
            (hq.at[q, cc], hs.at[q, cc]),
            (wq.at[slot, cc], ws.at[slot, cc]),
            w_send.at[q, cc],
            w_recv.at[slot, cc],
            (to, me_basis),
        )

    def w_arrival(cc, slot):
        return pair(
            (hq.at[slot, cc], hs.at[slot, cc]),
            (wq.at[slot, cc], ws.at[slot, cc]),
            w_send.at[slot, cc],
            w_recv.at[slot, cc],
            (lax.rem(me_grid + 1, grid_size), me_basis),
        )

    def w_from(slot):
        return lax.rem(me_grid * per_owner + slot * per, CL) // per

    for cc in range(per):
        for d in range(1, grid_size):
            for copy in z_copy(cc, d):
                copy.start()

    for cc in range(per):
        for d in range(1, grid_size):
            for copy in z_copy(cc, d):
                copy.wait_recv()
        for m in range(members):

            def add_up(i, carry):
                r = m * owned + i
                total = decode(kq[me_grid, cc, r], ks[me_grid, cc, pl.ds(r, 1), :])
                for d in range(1, grid_size):
                    total += decode(zq[d - 1, cc, r], zs[d - 1, cc, pl.ds(r, 1), :])
                sq[cc, m, i], ss[cc, m, pl.ds(i, 1), :] = encode(total)
                return carry

            lax.fori_loop(0, owned, add_up, 0)
        for d in range(1, basis_size):
            for copy in x_copy(cc, d):
                copy.start()

    for cc in range(per):
        for d in range(1, basis_size):
            for copy in x_copy(cc, d):
                copy.wait_recv()
        for q in range(turns):

            def place(i, carry):
                total = decode(
                    sq[cc, mine, i], ss[cc, mine, pl.ds(i, 1), :] * takes[0, cc, i, q : q + 1, :]
                )
                for d in range(1, basis_size):
                    total += decode(
                        xq[d - 1, cc, i],
                        xs[d - 1, cc, pl.ds(i, 1), :] * takes[d, cc, i, q : q + 1, :],
                    )
                hq[q, cc, i], hs[q, cc, pl.ds(i, 1), :] = encode(total)
                return carry

            lax.fori_loop(0, owned, place, 0)
            to, slot = w_place(q)

            @pl.when(to != me_grid)
            def _():
                for copy in w_copy(cc, q):
                    copy.start()

            @pl.when(to == me_grid)
            def _():
                wq[slot, cc] = hq[q, cc]
                ws[slot, cc] = hs[q, cc]

    for cc in range(per):
        for slot in range(turns):

            @pl.when(w_from(slot) != me_grid)
            def _():
                for copy in w_arrival(cc, slot):
                    copy.wait_recv()

            for i in range(owned):
                out[i * TB : (i + 1) * TB, (slot * per + cc) * TB : (slot * per + cc + 1) * TB] = (
                    decode(wq[slot, cc, i], ws[slot, cc, i : i + 1, :])
                )

    for cc in range(per):
        for d in range(1, grid_size):
            for copy in z_copy(cc, d):
                copy.wait_send()
        for d in range(1, basis_size):
            for copy in x_copy(cc, d):
                copy.wait_send()
        for q in range(turns):

            @pl.when(w_place(q)[0] != me_grid)
            def _():
                for copy in w_copy(cc, q):
                    copy.wait_send()


def collect(coded, scales, takes, grid_size, basis_size, owned, turns):
    per = CL // grid_size
    members = CL // owned
    vmem = pl.BlockSpec(memory_space=pltpu.VMEM)

    def both(*lead):
        return [
            pltpu.VMEM(lead + (TB, TB), jnp.int16),
            pltpu.VMEM(lead + (TB,), jnp.float32),
        ]

    return pl.pallas_call(
        functools.partial(collect_kernel, grid_size, basis_size, owned, turns),
        out_shape=jax.ShapeDtypeStruct((owned * TB, turns * per * TB), jnp.float32),
        in_specs=[vmem] * 3,
        out_specs=vmem,
        scratch_shapes=both(grid_size - 1, per, CL)
        + both(per, members, owned)
        + both(basis_size - 1, per, owned)
        + both(turns, per, owned)
        + both(turns, per, owned)
        + [
            pltpu.SemaphoreType.DMA((grid_size - 1, per, 2)),
            pltpu.SemaphoreType.DMA((grid_size - 1, per, 2)),
            pltpu.SemaphoreType.DMA((basis_size - 1, per, 2)),
            pltpu.SemaphoreType.DMA((basis_size - 1, per, 2)),
            pltpu.SemaphoreType.DMA((turns, per, 2)),
            pltpu.SemaphoreType.DMA((turns, per, 2)),
        ],
        compiler_params=pltpu.CompilerParams(
            collective_id=0, has_side_effects=True, vmem_limit_bytes=48 * 1024 * 1024
        ),
        name="collect",
    )(coded, scales, takes)


def body(
    basis_values,
    weights,
    points,
    block_lists,
    counts,
    density,
    centers,
    block_centers,
    block_exponents,
):
    basis_size = lax.axis_size("basis")
    grid_size = lax.axis_size("grid")
    me_basis = lax.axis_index("basis")
    me_grid = lax.axis_index("grid")
    block_count = block_exponents.shape[0]
    owned_blocks = block_count // basis_size
    turns = block_count // CL
    per = CL // grid_size
    batches, point_total = weights.shape
    lists = block_lists.shape[1]

    first = first_block_of(block_lists, block_count)
    firsts = lax.all_to_all(
        jnp.broadcast_to(first, (basis_size, 1)), "basis", split_axis=0, concat_axis=0, tiled=True
    )[:, 0]
    my_residues = me_grid * per + jnp.arange(per, dtype=jnp.int32)
    columns = block_with_residue(firsts[:, None], my_residues[None, :], block_count)

    packed = pack_density(columns, density, owned_blocks)
    tiles_in = lax.all_to_all(packed, "basis", split_axis=0, concat_axis=0, tiled=True)
    members = block_with_residue(first, jnp.arange(CL, dtype=jnp.int32), block_count)
    turn_of = members // CL
    chosen = (turn_of[None, :] == jnp.arange(turns, dtype=jnp.int32)[:, None])
    by_turn = tiles_in.reshape(turns, CL, per, TB, TB)
    mine = by_turn[0]
    for turn in range(1, turns):
        mine = jnp.where(chosen[turn][:, None, None, None], by_turn[turn], mine)
    dens = lax.all_to_all(
        jnp.broadcast_to(mine[None], (grid_size,) + mine.shape),
        "grid",
        split_axis=0,
        concat_axis=0,
        tiled=True,
    )

    coup = region_coupling(members, centers)
    boys = boys_table(
        points.astype(jnp.float32), block_lists, block_centers, block_exponents
    ).reshape(batches, lists * lists, point_total)
    live_count = counts[0, 0]
    is_live = jnp.arange(batches, dtype=jnp.int32) < live_count
    scaled = jnp.where(is_live[:, None], weights, 0.0) / point_total
    weighted = (basis_values * scaled[:, :, None]).astype(jnp.bfloat16)

    coded, scales = region_exchange(
        block_lists % CL, counts.reshape(1), basis_values, weighted, boys, dens, coup, grid_size
    )
    back = (me_basis - jnp.arange(basis_size, dtype=jnp.int32)) % basis_size
    begins = firsts[back]
    my_blocks = me_basis * owned_blocks + jnp.arange(owned_blocks, dtype=jnp.int32)
    inside = (my_blocks[None, :] - begins[:, None]) % block_count < CL
    turn_at = block_with_residue(begins[:, None], my_residues[None, :], block_count) // CL
    takes = (
        inside[:, None, :, None]
        & (turn_at[:, :, None, None] == jnp.arange(turns, dtype=jnp.int32)[None, None, None, :])
    )
    takes = jnp.broadcast_to(
        takes.astype(jnp.float32)[..., None], takes.shape + (TB,)
    )
    return collect(coded, scales, takes, grid_size, basis_size, owned_blocks, turns)


def solution(mesh):
    placed = (
        P(("grid", "basis"), None, None),
        P(("grid", "basis"), None),
        P(("grid", "basis"), None, None),
        P(("grid", "basis"), None),
        P("basis", "grid"),
        P("basis", None),
        P(),
        P(),
        P(),
    )
    return jax.shard_map(
        body, mesh=mesh, in_specs=placed, out_specs=P("basis", "grid"), check_vma=False
    )
```

```python
import functools
import math

import jax
import jax.numpy as jnp
from jax import lax
from jax.experimental import pallas as pl
from jax.experimental.pallas import tpu as pltpu
from jax.sharding import PartitionSpec as P

TB = 128
CL = 8


def boys_table(points_f, blocks, block_centers, block_exponents):
    centre = block_centers[:, blocks]
    middle = 0.5 * (centre[:, :, :, None] + centre[:, :, None, :])
    exponents = block_exponents[blocks]
    rate_pair = 0.5 * (exponents[:, :, None] + exponents[:, None, :])
    offset = points_f.transpose(1, 0, 2)[:, :, None, None, :] - middle[:, :, :, :, None]
    distance = jnp.sum(offset * offset, axis=0)
    tau_value = rate_pair[:, :, :, None] * distance + 0.05
    root_value = jnp.sqrt(tau_value)
    return 0.5 * math.sqrt(math.pi) * lax.erf(root_value) / root_value


def first_block_of(block_lists, block_count):
    present = jnp.any(
        block_lists.reshape(-1)[:, None] == jnp.arange(block_count, dtype=jnp.int32)[None, :],
        axis=0,
    )
    begins = present & jnp.logical_not(jnp.roll(present, 1))
    return jnp.sum(jnp.where(begins, jnp.arange(block_count, dtype=jnp.int32), 0))


def block_with_residue(first, residue, block_count):
    return (first + (residue - first) % CL) % block_count


def region_coupling(members, centers):
    functions = (members[:, None] * TB + jnp.arange(TB, dtype=jnp.int32)[None, :]).reshape(CL * TB)
    where_at = centers[:, functions].reshape(3, CL, TB)
    spread = where_at[:, :, None, :, None] - where_at[:, None, :, None, :]
    distance = jnp.sum(spread * spread, axis=0)
    sharpness = float(centers.shape[1]) ** (2.0 / 3.0)
    return jnp.exp(-sharpness * distance).astype(jnp.bfloat16)


def pack_kernel(column_ref, dens_ref, out_ref, sems):
    targets, per = out_ref.shape[:2]

    def copy(t, c):
        at = pl.multiple_of(column_ref[t, c] * TB, TB)
        return pltpu.make_async_copy(
            dens_ref.at[:, pl.ds(at, TB)], out_ref.at[t, c], sems.at[t, c]
        )

    for c in range(per):
        for t in range(targets):
            copy(t, c).start()
    for c in range(per):
        for t in range(targets):
            copy(t, c).wait()


def pack_density(columns, density):
    targets, per = columns.shape
    rows = density.shape[0]
    return pl.pallas_call(
        pack_kernel,
        in_specs=[
            pl.BlockSpec(memory_space=pltpu.SMEM),
            pl.BlockSpec(memory_space=pl.ANY),
        ],
        out_specs=pl.BlockSpec(memory_space=pltpu.VMEM),
        out_shape=jax.ShapeDtypeStruct((targets, per, rows, TB), jnp.bfloat16),
        scratch_shapes=[pltpu.SemaphoreType.DMA((targets, per))],
        name="pack_density",
    )(columns, density)


def fetch_kernel(grid_size, basis_size, owned, slot_ref, packed, out, *scratch):
    per = CL // grid_size
    landed = scratch[:per]
    x_send, x_recv, z_send, z_recv = scratch[per:]
    me_grid = lax.axis_index("grid")
    me_basis = lax.axis_index("basis")
    mesh_ids = pl.DeviceIdType.MESH

    barrier = pltpu.get_barrier_semaphore()
    for d in (1, grid_size - 1):
        pl.semaphore_signal(
            barrier,
            inc=1,
            device_id=(lax.rem(me_grid + d, grid_size), me_basis),
            device_id_type=mesh_ids,
        )
    for d in range(1, basis_size):
        pl.semaphore_signal(
            barrier,
            inc=1,
            device_id=(me_grid, lax.rem(me_basis + d, basis_size)),
            device_id_type=mesh_ids,
        )
    pl.semaphore_wait(barrier, basis_size + 1)

    def x_copy(cc, d):
        to = lax.rem(me_basis + d, basis_size)
        return pltpu.make_async_remote_copy(
            src_ref=packed.at[to, cc],
            dst_ref=landed[cc].at[d],
            send_sem=x_send.at[d - 1, cc],
            recv_sem=x_recv.at[d - 1, cc],
            device_id=(me_grid, to),
            device_id_type=mesh_ids,
        )

    def z_copy(cc, j, side):
        step = 1 if side == 0 else grid_size - 1
        return pltpu.make_async_remote_copy(
            src_ref=out.at[j, cc],
            dst_ref=out.at[j, cc],
            send_sem=z_send.at[j, cc, side],
            recv_sem=z_recv.at[j, cc],
            device_id=(lax.rem(me_grid + step, grid_size), me_basis),
            device_id_type=mesh_ids,
        )

    def own(cc):
        landed[cc][0] = packed[me_basis, cc]
        for d in range(1, basis_size):
            x_copy(cc, d).wait_recv()
        for r in range(CL):
            out[me_grid, cc, r] = landed[cc][
                slot_ref[r], (r % owned) * TB : (r % owned + 1) * TB, :
            ]

        @pl.when(me_grid < grid_size - 1)
        def _():
            z_copy(cc, me_grid, 0).start()

        @pl.when(me_grid > 0)
        def _():
            z_copy(cc, me_grid, 1).start()

    def relay(cc, h):
        @pl.when(me_grid >= h)
        def _():
            z_copy(cc, me_grid - h, 0).wait_recv()

            @pl.when(me_grid < grid_size - 1)
            def _():
                z_copy(cc, me_grid - h, 0).start()

        @pl.when(me_grid + h < grid_size)
        def _():
            z_copy(cc, me_grid + h, 1).wait_recv()

            @pl.when(me_grid > 0)
            def _():
                z_copy(cc, me_grid + h, 1).start()

    for cc in range(per):
        for d in range(1, basis_size):
            x_copy(cc, d).start()
    for cc in range(per):
        own(cc)
        if grid_size > 1:
            relay(cc, 1)
    for h in range(2, grid_size):
        for cc in range(per):
            relay(cc, h)

    for cc in range(per):
        for d in range(1, basis_size):
            x_copy(cc, d).wait_send()
        for h in range(grid_size):

            @pl.when((me_grid >= h) & (me_grid < grid_size - 1))
            def _():
                z_copy(cc, me_grid - h, 0).wait_send()

            @pl.when((me_grid + h < grid_size) & (me_grid > 0))
            def _():
                z_copy(cc, me_grid + h, 1).wait_send()


def fetch_density(slots, packed, grid_size, basis_size, owned):
    per = CL // grid_size
    vmem = pl.BlockSpec(memory_space=pltpu.VMEM)
    return pl.pallas_call(
        functools.partial(fetch_kernel, grid_size, basis_size, owned),
        out_shape=jax.ShapeDtypeStruct((grid_size, per, CL, TB, TB), jnp.bfloat16),
        in_specs=[pl.BlockSpec(memory_space=pltpu.SMEM), vmem],
        out_specs=vmem,
        scratch_shapes=[pltpu.VMEM((basis_size, owned * TB, TB), jnp.bfloat16)] * per
        + [
            pltpu.SemaphoreType.DMA((basis_size - 1, per)),
            pltpu.SemaphoreType.DMA((basis_size - 1, per)),
            pltpu.SemaphoreType.DMA((grid_size, per, 2)),
            pltpu.SemaphoreType.DMA((grid_size, per)),
        ],
        compiler_params=pltpu.CompilerParams(
            collective_id=1, has_side_effects=True, vmem_limit_bytes=32 * 1024 * 1024
        ),
        name="fetch_density",
    )(slots, packed)


def encode(tile):
    top = jnp.maximum(jnp.max(jnp.abs(tile), axis=0, keepdims=True), 1e-30)
    steps = jnp.round(tile * (32767.0 / top))
    return steps.astype(jnp.int32).astype(jnp.int16), top * (1.0 / 32767.0)


def decode(coded, scale):
    return coded.astype(jnp.int32).astype(jnp.float32) * scale


def batch_kernel(
    per, place_ref, count_ref, values_ref, weighted_ref, boys_ref, dens_ref, coup_ref, out_ref, scale_ref, acc
):
    n = pl.program_id(0)
    lists = place_ref.shape[1]

    @pl.when(n == 0)
    def _():
        acc[...] = jnp.zeros_like(acc)

    @pl.when(n < count_ref[0])
    def _():
        at = [place_ref[n, t] for t in range(lists)]
        dens = jnp.concatenate(
            [
                jnp.concatenate([dens_ref[c // per, c % per, r] for c in at], axis=1)
                for r in at
            ],
            axis=0,
        )
        mapped = lax.dot_general(
            dens, values_ref[0], (((1,), (1,)), ((), ())), preferred_element_type=jnp.float32
        ).astype(jnp.bfloat16)
        total = None
        for u in range(lists):
            coup = jnp.concatenate([coup_ref[r, at[u]] for r in at], axis=0)
            part = jnp.dot(
                coup, mapped[u * TB : (u + 1) * TB], preferred_element_type=jnp.float32
            )
            part = jnp.concatenate(
                [
                    part[t * TB : (t + 1) * TB]
                    * boys_ref[0, t * lists + u : t * lists + u + 1, :]
                    for t in range(lists)
                ],
                axis=0,
            )
            total = part if total is None else total + part
        tile = jnp.dot(
            total.astype(jnp.bfloat16), weighted_ref[0], preferred_element_type=jnp.float32
        )
        for c in range(lists):
            for r in range(lists):
                acc[at[c], at[r]] += tile[c * TB : (c + 1) * TB, r * TB : (r + 1) * TB]

    @pl.when(n == pl.num_programs(0) - 1)
    def _():
        def put(index, carry):
            c = index // CL
            r = index % CL
            coded, scale = encode(acc[c, r].T)
            out_ref[c // per, c % per, r] = coded
            scale_ref[c // per, c % per, pl.ds(r, 1), :] = scale
            return carry

        lax.fori_loop(0, CL * CL, put, 0)


def region_exchange(places, count, values, weighted, boys, dens, coup, grid_size):
    batches, points, listed = values.shape
    per = CL // grid_size
    lists = places.shape[1]
    whole = lambda *shape: pl.BlockSpec(shape, lambda n, *_: (0,) * len(shape))
    return pl.pallas_call(
        functools.partial(batch_kernel, per),
        grid_spec=pltpu.PrefetchScalarGridSpec(
            num_scalar_prefetch=2,
            grid=(batches,),
            in_specs=[
                pl.BlockSpec((1, points, listed), lambda n, *_: (n, 0, 0)),
                pl.BlockSpec((1, points, listed), lambda n, *_: (n, 0, 0)),
                pl.BlockSpec((1, lists * lists, points), lambda n, *_: (n, 0, 0)),
                whole(grid_size, per, CL, TB, TB),
                whole(CL, CL, TB, TB),
            ],
            out_specs=[
                whole(grid_size, per, CL, TB, TB),
                whole(grid_size, per, CL, TB),
            ],
            scratch_shapes=[pltpu.VMEM((CL, CL, TB, TB), jnp.float32)],
        ),
        out_shape=[
            jax.ShapeDtypeStruct((grid_size, per, CL, TB, TB), jnp.int16),
            jax.ShapeDtypeStruct((grid_size, per, CL, TB), jnp.float32),
        ],
        compiler_params=pltpu.CompilerParams(vmem_limit_bytes=48 * 1024 * 1024),
        name="region_exchange",
    )(places, count, values, weighted, boys, dens, coup)


def collect_kernel(
    grid_size,
    basis_size,
    owned,
    turns,
    kq,
    ks,
    takes,
    out,
    zq,
    zs,
    sq,
    ss,
    xq,
    xs,
    hq,
    hs,
    wq,
    ws,
    z_send,
    z_recv,
    x_send,
    x_recv,
    w_send,
    w_recv,
):
    per = CL // grid_size
    members = CL // owned
    per_owner = turns * per
    me_grid = lax.axis_index("grid")
    me_basis = lax.axis_index("basis")
    mine = lax.rem(me_basis, members)

    barrier = pltpu.get_barrier_semaphore()
    for d in range(1, grid_size):
        pl.semaphore_signal(
            barrier,
            inc=1,
            device_id=(lax.rem(me_grid + d, grid_size), me_basis),
            device_id_type=pl.DeviceIdType.MESH,
        )
    for d in range(1, basis_size):
        pl.semaphore_signal(
            barrier,
            inc=1,
            device_id=(me_grid, lax.rem(me_basis + d, basis_size)),
            device_id_type=pl.DeviceIdType.MESH,
        )
    pl.semaphore_wait(barrier, grid_size + basis_size - 2)

    def pair(sources, targets, sends, recvs, device):
        return [
            pltpu.make_async_remote_copy(
                src_ref=sources[which],
                dst_ref=targets[which],
                send_sem=sends.at[which],
                recv_sem=recvs.at[which],
                device_id=device,
                device_id_type=pl.DeviceIdType.MESH,
            )
            for which in range(2)
        ]

    def z_copy(cc, d):
        to = lax.rem(me_grid + d, grid_size)
        return pair(
            (kq.at[to, cc], ks.at[to, cc]),
            (zq.at[d - 1, cc], zs.at[d - 1, cc]),
            z_send.at[d - 1, cc],
            z_recv.at[d - 1, cc],
            (to, me_basis),
        )

    def x_copy(cc, d):
        to = lax.rem(me_basis + d, basis_size)
        its = lax.rem(to, members)
        return pair(
            (sq.at[cc, its], ss.at[cc, its]),
            (xq.at[d - 1, cc], xs.at[d - 1, cc]),
            x_send.at[d - 1, cc],
            x_recv.at[d - 1, cc],
            (me_grid, to),
        )

    def w_place(q):
        at = CL * q + me_grid * per
        return at // per_owner, lax.rem(at, per_owner) // per

    def w_copy(cc, q):
        to, slot = w_place(q)
        return pair(
            (hq.at[q, cc], hs.at[q, cc]),
            (wq.at[slot, cc], ws.at[slot, cc]),
            w_send.at[q, cc],
            w_recv.at[slot, cc],
            (to, me_basis),
        )

    def w_arrival(cc, slot):
        return pair(
            (hq.at[slot, cc], hs.at[slot, cc]),
            (wq.at[slot, cc], ws.at[slot, cc]),
            w_send.at[slot, cc],
            w_recv.at[slot, cc],
            (lax.rem(me_grid + 1, grid_size), me_basis),
        )

    def w_from(slot):
        return lax.rem(me_grid * per_owner + slot * per, CL) // per

    for cc in range(per):
        for d in range(1, grid_size):
            for copy in z_copy(cc, d):
                copy.start()

    for cc in range(per):
        for d in range(1, grid_size):
            for copy in z_copy(cc, d):
                copy.wait_recv()
        for m in range(members):

            def add_up(i, carry):
                r = m * owned + i
                total = decode(kq[me_grid, cc, r], ks[me_grid, cc, pl.ds(r, 1), :])
                for d in range(1, grid_size):
                    total += decode(zq[d - 1, cc, r], zs[d - 1, cc, pl.ds(r, 1), :])
                sq[cc, m, i], ss[cc, m, pl.ds(i, 1), :] = encode(total)
                return carry

            lax.fori_loop(0, owned, add_up, 0)
        for d in range(1, basis_size):
            for copy in x_copy(cc, d):
                copy.start()

    for cc in range(per):
        for d in range(1, basis_size):
            for copy in x_copy(cc, d):
                copy.wait_recv()
        for q in range(turns):

            def place(i, carry):
                total = decode(
                    sq[cc, mine, i], ss[cc, mine, pl.ds(i, 1), :] * takes[0, cc, i, q : q + 1, :]
                )
                for d in range(1, basis_size):
                    total += decode(
                        xq[d - 1, cc, i],
                        xs[d - 1, cc, pl.ds(i, 1), :] * takes[d, cc, i, q : q + 1, :],
                    )
                hq[q, cc, i], hs[q, cc, pl.ds(i, 1), :] = encode(total)
                return carry

            lax.fori_loop(0, owned, place, 0)
            to, slot = w_place(q)

            @pl.when(to != me_grid)
            def _():
                for copy in w_copy(cc, q):
                    copy.start()

            @pl.when(to == me_grid)
            def _():
                wq[slot, cc] = hq[q, cc]
                ws[slot, cc] = hs[q, cc]

    for cc in range(per):
        for slot in range(turns):

            @pl.when(w_from(slot) != me_grid)
            def _():
                for copy in w_arrival(cc, slot):
                    copy.wait_recv()

            for i in range(owned):
                out[i * TB : (i + 1) * TB, (slot * per + cc) * TB : (slot * per + cc + 1) * TB] = (
                    decode(wq[slot, cc, i], ws[slot, cc, i : i + 1, :])
                )

    for cc in range(per):
        for d in range(1, grid_size):
            for copy in z_copy(cc, d):
                copy.wait_send()
        for d in range(1, basis_size):
            for copy in x_copy(cc, d):
                copy.wait_send()
        for q in range(turns):

            @pl.when(w_place(q)[0] != me_grid)
            def _():
                for copy in w_copy(cc, q):
                    copy.wait_send()


def collect(coded, scales, takes, grid_size, basis_size, owned, turns):
    per = CL // grid_size
    members = CL // owned
    vmem = pl.BlockSpec(memory_space=pltpu.VMEM)

    def both(*lead):
        return [
            pltpu.VMEM(lead + (TB, TB), jnp.int16),
            pltpu.VMEM(lead + (TB,), jnp.float32),
        ]

    return pl.pallas_call(
        functools.partial(collect_kernel, grid_size, basis_size, owned, turns),
        out_shape=jax.ShapeDtypeStruct((owned * TB, turns * per * TB), jnp.float32),
        in_specs=[vmem] * 3,
        out_specs=vmem,
        scratch_shapes=both(grid_size - 1, per, CL)
        + both(per, members, owned)
        + both(basis_size - 1, per, owned)
        + both(turns, per, owned)
        + both(turns, per, owned)
        + [
            pltpu.SemaphoreType.DMA((grid_size - 1, per, 2)),
            pltpu.SemaphoreType.DMA((grid_size - 1, per, 2)),
            pltpu.SemaphoreType.DMA((basis_size - 1, per, 2)),
            pltpu.SemaphoreType.DMA((basis_size - 1, per, 2)),
            pltpu.SemaphoreType.DMA((turns, per, 2)),
            pltpu.SemaphoreType.DMA((turns, per, 2)),
        ],
        compiler_params=pltpu.CompilerParams(
            collective_id=0, has_side_effects=True, vmem_limit_bytes=48 * 1024 * 1024
        ),
        name="collect",
    )(coded, scales, takes)


def body(
    basis_values,
    weights,
    points,
    block_lists,
    counts,
    density,
    centers,
    block_centers,
    block_exponents,
):
    basis_size = lax.axis_size("basis")
    grid_size = lax.axis_size("grid")
    me_basis = lax.axis_index("basis")
    me_grid = lax.axis_index("grid")
    block_count = block_exponents.shape[0]
    owned_blocks = block_count // basis_size
    turns = block_count // CL
    per = CL // grid_size
    batches, point_total = weights.shape
    lists = block_lists.shape[1]

    first = first_block_of(block_lists, block_count)
    firsts = lax.all_to_all(
        jnp.broadcast_to(first, (basis_size, 1)), "basis", split_axis=0, concat_axis=0, tiled=True
    )[:, 0]
    my_residues = me_grid * per + jnp.arange(per, dtype=jnp.int32)
    columns = block_with_residue(firsts[:, None], my_residues[None, :], block_count)

    members = block_with_residue(first, jnp.arange(CL, dtype=jnp.int32), block_count)
    slots = (me_basis - members // owned_blocks) % basis_size

    coup = region_coupling(members, centers)
    boys = boys_table(
        points.astype(jnp.float32), block_lists, block_centers, block_exponents
    ).reshape(batches, lists * lists, point_total)
    live_count = counts[0, 0]
    is_live = jnp.arange(batches, dtype=jnp.int32) < live_count
    scaled = jnp.where(is_live[:, None], weights, 0.0) / point_total
    weighted = (basis_values * scaled[:, :, None]).astype(jnp.bfloat16)

    packed = pack_density(columns, density)
    dens = fetch_density(slots, packed, grid_size, basis_size, owned_blocks)
    coded, scales = region_exchange(
        block_lists % CL, counts.reshape(1), basis_values, weighted, boys, dens, coup, grid_size
    )
    back = (me_basis - jnp.arange(basis_size, dtype=jnp.int32)) % basis_size
    begins = firsts[back]
    my_blocks = me_basis * owned_blocks + jnp.arange(owned_blocks, dtype=jnp.int32)
    inside = (my_blocks[None, :] - begins[:, None]) % block_count < CL
    turn_at = block_with_residue(begins[:, None], my_residues[None, :], block_count) // CL
    takes = (
        inside[:, None, :, None]
        & (turn_at[:, :, None, None] == jnp.arange(turns, dtype=jnp.int32)[None, None, None, :])
    )
    takes = jnp.broadcast_to(
        takes.astype(jnp.float32)[..., None], takes.shape + (TB,)
    )
    return collect(coded, scales, takes, grid_size, basis_size, owned_blocks, turns)


def solution(mesh):
    placed = (
        P(("grid", "basis"), None, None),
        P(("grid", "basis"), None),
        P(("grid", "basis"), None, None),
        P(("grid", "basis"), None),
        P("basis", "grid"),
        P("basis", None),
        P(),
        P(),
        P(),
    )
    return jax.shard_map(
        body, mesh=mesh, in_specs=placed, out_specs=P("basis", "grid"), check_vma=False
    )
```

```python
import functools
import math

import jax
import jax.numpy as jnp
from jax import lax
from jax.experimental import pallas as pl
from jax.experimental.pallas import tpu as pltpu
from jax.sharding import PartitionSpec as P

TB = 128
CL = 8


def boys_table(points_f, blocks, block_centers, block_exponents):
    centre = block_centers[:, blocks]
    middle = 0.5 * (centre[:, :, :, None] + centre[:, :, None, :])
    exponents = block_exponents[blocks]
    rate_pair = 0.5 * (exponents[:, :, None] + exponents[:, None, :])
    offset = points_f.transpose(1, 0, 2)[:, :, None, None, :] - middle[:, :, :, :, None]
    distance = jnp.sum(offset * offset, axis=0)
    tau_value = rate_pair[:, :, :, None] * distance + 0.05
    root_value = jnp.sqrt(tau_value)
    return 0.5 * math.sqrt(math.pi) * lax.erf(root_value) / root_value


def first_block_of(block_lists, block_count):
    present = jnp.any(
        block_lists.reshape(-1)[:, None] == jnp.arange(block_count, dtype=jnp.int32)[None, :],
        axis=0,
    )
    begins = present & jnp.logical_not(jnp.roll(present, 1))
    return jnp.sum(jnp.where(begins, jnp.arange(block_count, dtype=jnp.int32), 0))


def block_with_residue(first, residue, block_count):
    return (first + (residue - first) % CL) % block_count


def region_coupling(members, centers):
    functions = (members[:, None] * TB + jnp.arange(TB, dtype=jnp.int32)[None, :]).reshape(CL * TB)
    where_at = centers[:, functions].reshape(3, CL, TB)
    spread = where_at[:, :, None, :, None] - where_at[:, None, :, None, :]
    distance = jnp.sum(spread * spread, axis=0)
    sharpness = float(centers.shape[1]) ** (2.0 / 3.0)
    return jnp.exp(-sharpness * distance).astype(jnp.bfloat16)


def pack_kernel(column_ref, dens_ref, out_ref, sems):
    targets, per = out_ref.shape[:2]

    def copy(t, c):
        at = pl.multiple_of(column_ref[t, c] * TB, TB)
        return pltpu.make_async_copy(
            dens_ref.at[:, pl.ds(at, TB)], out_ref.at[t, c], sems.at[t, c]
        )

    for c in range(per):
        for t in range(targets):
            copy(t, c).start()
    for c in range(per):
        for t in range(targets):
            copy(t, c).wait()


def pack_density(columns, density):
    targets, per = columns.shape
    rows = density.shape[0]
    return pl.pallas_call(
        pack_kernel,
        in_specs=[
            pl.BlockSpec(memory_space=pltpu.SMEM),
            pl.BlockSpec(memory_space=pl.ANY),
        ],
        out_specs=pl.BlockSpec(memory_space=pltpu.VMEM),
        out_shape=jax.ShapeDtypeStruct((targets, per, rows, TB), jnp.bfloat16),
        scratch_shapes=[pltpu.SemaphoreType.DMA((targets, per))],
        name="pack_density",
    )(columns, density)


def fetch_kernel(grid_size, basis_size, owned, slot_ref, packed, out, *scratch):
    per = CL // grid_size
    landed = scratch[:per]
    x_send, x_recv, z_send, z_recv = scratch[per:]
    me_grid = lax.axis_index("grid")
    me_basis = lax.axis_index("basis")
    mesh_ids = pl.DeviceIdType.MESH

    barrier = pltpu.get_barrier_semaphore()
    for d in (1, grid_size - 1):
        pl.semaphore_signal(
            barrier,
            inc=1,
            device_id=(lax.rem(me_grid + d, grid_size), me_basis),
            device_id_type=mesh_ids,
        )
    for d in range(1, basis_size):
        pl.semaphore_signal(
            barrier,
            inc=1,
            device_id=(me_grid, lax.rem(me_basis + d, basis_size)),
            device_id_type=mesh_ids,
        )
    pl.semaphore_wait(barrier, basis_size + 1)

    def x_copy(cc, d):
        to = lax.rem(me_basis + d, basis_size)
        return pltpu.make_async_remote_copy(
            src_ref=packed.at[to, cc],
            dst_ref=landed[cc].at[d],
            send_sem=x_send.at[d - 1, cc],
            recv_sem=x_recv.at[d - 1, cc],
            device_id=(me_grid, to),
            device_id_type=mesh_ids,
        )

    def z_copy(cc, j, side):
        step = 1 if side == 0 else grid_size - 1
        return pltpu.make_async_remote_copy(
            src_ref=out.at[j, cc],
            dst_ref=out.at[j, cc],
            send_sem=z_send.at[j, cc, side],
            recv_sem=z_recv.at[j, cc],
            device_id=(lax.rem(me_grid + step, grid_size), me_basis),
            device_id_type=mesh_ids,
        )

    def own(cc):
        landed[cc][0] = packed[me_basis, cc]
        for d in range(1, basis_size):
            x_copy(cc, d).wait_recv()
        for r in range(CL):
            out[me_grid, cc, r] = landed[cc][
                slot_ref[r], (r % owned) * TB : (r % owned + 1) * TB, :
            ]

        @pl.when(me_grid < grid_size - 1)
        def _():
            z_copy(cc, me_grid, 0).start()

        @pl.when(me_grid > 0)
        def _():
            z_copy(cc, me_grid, 1).start()

    def relay(cc, h):
        @pl.when(me_grid >= h)
        def _():
            z_copy(cc, me_grid - h, 0).wait_recv()

            @pl.when(me_grid < grid_size - 1)
            def _():
                z_copy(cc, me_grid - h, 0).start()

        @pl.when(me_grid + h < grid_size)
        def _():
            z_copy(cc, me_grid + h, 1).wait_recv()

            @pl.when(me_grid > 0)
            def _():
                z_copy(cc, me_grid + h, 1).start()

    for cc in range(per):
        for d in range(1, basis_size):
            x_copy(cc, d).start()
    for cc in range(per):
        own(cc)
        if grid_size > 1:
            relay(cc, 1)
    for h in range(2, grid_size):
        for cc in range(per):
            relay(cc, h)

    for cc in range(per):
        for d in range(1, basis_size):
            x_copy(cc, d).wait_send()
        for h in range(grid_size):

            @pl.when((me_grid >= h) & (me_grid < grid_size - 1))
            def _():
                z_copy(cc, me_grid - h, 0).wait_send()

            @pl.when((me_grid + h < grid_size) & (me_grid > 0))
            def _():
                z_copy(cc, me_grid + h, 1).wait_send()


def fetch_density(slots, packed, grid_size, basis_size, owned):
    per = CL // grid_size
    vmem = pl.BlockSpec(memory_space=pltpu.VMEM)
    return pl.pallas_call(
        functools.partial(fetch_kernel, grid_size, basis_size, owned),
        out_shape=jax.ShapeDtypeStruct((grid_size, per, CL, TB, TB), jnp.bfloat16),
        in_specs=[pl.BlockSpec(memory_space=pltpu.SMEM), vmem],
        out_specs=vmem,
        scratch_shapes=[pltpu.VMEM((basis_size, owned * TB, TB), jnp.bfloat16)] * per
        + [
            pltpu.SemaphoreType.DMA((basis_size - 1, per)),
            pltpu.SemaphoreType.DMA((basis_size - 1, per)),
            pltpu.SemaphoreType.DMA((grid_size, per, 2)),
            pltpu.SemaphoreType.DMA((grid_size, per)),
        ],
        compiler_params=pltpu.CompilerParams(
            collective_id=1, has_side_effects=True, vmem_limit_bytes=32 * 1024 * 1024
        ),
        name="fetch_density",
    )(slots, packed)


def encode(tile):
    top = jnp.maximum(jnp.max(jnp.abs(tile), axis=0, keepdims=True), 1e-30)
    steps = jnp.round(tile * (32767.0 / top))
    return steps.astype(jnp.int32).astype(jnp.int16), top * (1.0 / 32767.0)


def decode(coded, scale):
    return coded.astype(jnp.int32).astype(jnp.float32) * scale


def batch_kernel(
    per, place_ref, count_ref, values_ref, weighted_ref, boys_ref, dens_ref, coup_ref, out_ref, scale_ref, acc
):
    n = pl.program_id(0)
    lists = place_ref.shape[1]
    group = values_ref.shape[0]

    @pl.when(n == 0)
    def _():
        acc[...] = jnp.zeros_like(acc)

    def one(b):
        at = [place_ref[n * group + b, t] for t in range(lists)]
        dens = jnp.concatenate(
            [
                jnp.concatenate([dens_ref[c // per, c % per, r] for c in at], axis=1)
                for r in at
            ],
            axis=0,
        )
        mapped = lax.dot_general(
            dens, values_ref[b], (((1,), (1,)), ((), ())), preferred_element_type=jnp.float32
        ).astype(jnp.bfloat16)
        total = None
        for u in range(lists):
            coup = jnp.concatenate([coup_ref[r, at[u]] for r in at], axis=0)
            part = jnp.dot(
                coup, mapped[u * TB : (u + 1) * TB], preferred_element_type=jnp.float32
            )
            part = jnp.concatenate(
                [
                    part[t * TB : (t + 1) * TB]
                    * boys_ref[b, t * lists + u : t * lists + u + 1, :]
                    for t in range(lists)
                ],
                axis=0,
            )
            total = part if total is None else total + part
        tile = jnp.dot(
            total.astype(jnp.bfloat16), weighted_ref[b], preferred_element_type=jnp.float32
        )
        return at, tile

    @pl.when(n * group < count_ref[0])
    def _():
        for at, tile in [one(b) for b in range(group)]:
            for c in range(lists):
                for r in range(lists):
                    acc[at[c], at[r]] += tile[c * TB : (c + 1) * TB, r * TB : (r + 1) * TB]

    @pl.when(n == pl.num_programs(0) - 1)
    def _():
        def put(index, carry):
            c = index // CL
            r = index % CL
            coded, scale = encode(acc[c, r].T)
            out_ref[c // per, c % per, r] = coded
            scale_ref[c // per, c % per, pl.ds(r, 1), :] = scale
            return carry

        lax.fori_loop(0, CL * CL, put, 0)


def region_exchange(places, count, values, weighted, boys, dens, coup, grid_size):
    batches, points, listed = values.shape
    per = CL // grid_size
    lists = places.shape[1]
    group = math.gcd(batches, 2)
    whole = lambda *shape: pl.BlockSpec(shape, lambda n, *_: (0,) * len(shape))
    return pl.pallas_call(
        functools.partial(batch_kernel, per),
        grid_spec=pltpu.PrefetchScalarGridSpec(
            num_scalar_prefetch=2,
            grid=(batches // group,),
            in_specs=[
                pl.BlockSpec((group, points, listed), lambda n, *_: (n, 0, 0)),
                pl.BlockSpec((group, points, listed), lambda n, *_: (n, 0, 0)),
                pl.BlockSpec((group, lists * lists, points), lambda n, *_: (n, 0, 0)),
                whole(grid_size, per, CL, TB, TB),
                whole(CL, CL, TB, TB),
            ],
            out_specs=[
                whole(grid_size, per, CL, TB, TB),
                whole(grid_size, per, CL, TB),
            ],
            scratch_shapes=[pltpu.VMEM((CL, CL, TB, TB), jnp.float32)],
        ),
        out_shape=[
            jax.ShapeDtypeStruct((grid_size, per, CL, TB, TB), jnp.int16),
            jax.ShapeDtypeStruct((grid_size, per, CL, TB), jnp.float32),
        ],
        compiler_params=pltpu.CompilerParams(vmem_limit_bytes=48 * 1024 * 1024),
        name="region_exchange",
    )(places, count, values, weighted, boys, dens, coup)


def collect_kernel(
    grid_size,
    basis_size,
    owned,
    turns,
    kq,
    ks,
    takes,
    out,
    zq,
    zs,
    yq,
    ys,
    sq,
    ss,
    xq,
    xs,
    hq,
    hs,
    wq,
    ws,
    z_send,
    z_recv,
    x_send,
    x_recv,
    w_send,
    w_recv,
):
    per = CL // grid_size
    members = CL // owned
    per_owner = turns * per
    me_grid = lax.axis_index("grid")
    me_basis = lax.axis_index("basis")
    mine = lax.rem(me_basis, members)

    barrier = pltpu.get_barrier_semaphore()
    for d in range(1, grid_size):
        pl.semaphore_signal(
            barrier,
            inc=1,
            device_id=(lax.rem(me_grid + d, grid_size), me_basis),
            device_id_type=pl.DeviceIdType.MESH,
        )
    for d in range(1, basis_size):
        pl.semaphore_signal(
            barrier,
            inc=1,
            device_id=(me_grid, lax.rem(me_basis + d, basis_size)),
            device_id_type=pl.DeviceIdType.MESH,
        )
    pl.semaphore_wait(barrier, grid_size + basis_size - 2)

    def pair(sources, targets, sends, recvs, device):
        return [
            pltpu.make_async_remote_copy(
                src_ref=sources[which],
                dst_ref=targets[which],
                send_sem=sends.at[which],
                recv_sem=recvs.at[which],
                device_id=device,
                device_id_type=pl.DeviceIdType.MESH,
            )
            for which in range(2)
        ]

    def z_copy(cc, j, side, fresh):
        to = lax.rem(me_grid + (1 if side == 0 else grid_size - 1), grid_size)
        return pair(
            (kq.at[j, cc], ks.at[j, cc]) if fresh else (yq.at[side, j, cc], ys.at[side, j, cc]),
            (zq.at[side, j, cc], zs.at[side, j, cc]),
            z_send.at[side, j, cc],
            z_recv.at[side, j, cc],
            (to, me_basis),
        )

    last = grid_size - 1

    def pass_on(cc, j, side):
        more = (me_grid > 0) & (me_grid < j) if side == 0 else (me_grid < last) & (me_grid > j)

        @pl.when(more)
        def _():
            for copy in z_copy(cc, j, side, False):
                copy.wait_recv()

            def add_own(r, carry):
                row = pl.ds(r, 1)
                yq[side, j, cc, r], ys[side, j, cc, row, :] = encode(
                    decode(kq[j, cc, r], ks[j, cc, row, :])
                    + decode(zq[side, j, cc, r], zs[side, j, cc, row, :])
                )
                return carry

            lax.fori_loop(0, CL, add_own, 0)
            for copy in z_copy(cc, j, side, False):
                copy.start()

    def x_copy(cc, d):
        to = lax.rem(me_basis + d, basis_size)
        its = lax.rem(to, members)
        return pair(
            (sq.at[cc, its], ss.at[cc, its]),
            (xq.at[d - 1, cc], xs.at[d - 1, cc]),
            x_send.at[d - 1, cc],
            x_recv.at[d - 1, cc],
            (me_grid, to),
        )

    def w_place(q):
        at = CL * q + me_grid * per
        return at // per_owner, lax.rem(at, per_owner) // per

    def w_copy(cc, q):
        to, slot = w_place(q)
        return pair(
            (hq.at[q, cc], hs.at[q, cc]),
            (wq.at[slot, cc], ws.at[slot, cc]),
            w_send.at[q, cc],
            w_recv.at[slot, cc],
            (to, me_basis),
        )

    def w_arrival(cc, slot):
        return pair(
            (hq.at[slot, cc], hs.at[slot, cc]),
            (wq.at[slot, cc], ws.at[slot, cc]),
            w_send.at[slot, cc],
            w_recv.at[slot, cc],
            (lax.rem(me_grid + 1, grid_size), me_basis),
        )

    def w_from(slot):
        return lax.rem(me_grid * per_owner + slot * per, CL) // per

    @pl.when(me_grid == 0)
    def _():
        for cc in range(per):
            for j in range(last, 0, -1):
                for copy in z_copy(cc, j, 0, True):
                    copy.start()
        zq[0, 0] = jnp.zeros(zq.shape[2:], zq.dtype)
        zs[0, 0] = jnp.zeros(zs.shape[2:], zs.dtype)

    @pl.when(me_grid == last)
    def _():
        for cc in range(per):
            for j in range(last):
                for copy in z_copy(cc, j, 1, True):
                    copy.start()
        zq[1, last] = jnp.zeros(zq.shape[2:], zq.dtype)
        zs[1, last] = jnp.zeros(zs.shape[2:], zs.dtype)

    for cc in range(per):
        for k in range(last):
            pass_on(cc, last - k, 0)
            pass_on(cc, k, 1)

        @pl.when(me_grid > 0)
        def _():
            for copy in z_copy(cc, me_grid, 0, False):
                copy.wait_recv()

        @pl.when(me_grid < last)
        def _():
            for copy in z_copy(cc, me_grid, 1, False):
                copy.wait_recv()

        for m in range(members):

            def add_up(i, carry):
                r = m * owned + i
                total = decode(kq[me_grid, cc, r], ks[me_grid, cc, pl.ds(r, 1), :])
                for side in range(2):
                    total += decode(
                        zq[side, me_grid, cc, r], zs[side, me_grid, cc, pl.ds(r, 1), :]
                    )
                sq[cc, m, i], ss[cc, m, pl.ds(i, 1), :] = encode(total)
                return carry

            lax.fori_loop(0, owned, add_up, 0)
        for d in range(1, basis_size):
            for copy in x_copy(cc, d):
                copy.start()

    for cc in range(per):
        for d in range(1, basis_size):
            for copy in x_copy(cc, d):
                copy.wait_recv()
        for q in range(turns):

            def place(i, carry):
                total = decode(
                    sq[cc, mine, i], ss[cc, mine, pl.ds(i, 1), :] * takes[0, cc, i, q : q + 1, :]
                )
                for d in range(1, basis_size):
                    total += decode(
                        xq[d - 1, cc, i],
                        xs[d - 1, cc, pl.ds(i, 1), :] * takes[d, cc, i, q : q + 1, :],
                    )
                hq[q, cc, i], hs[q, cc, pl.ds(i, 1), :] = encode(total)
                return carry

            lax.fori_loop(0, owned, place, 0)
            to, slot = w_place(q)

            @pl.when(to != me_grid)
            def _():
                for copy in w_copy(cc, q):
                    copy.start()

            @pl.when(to == me_grid)
            def _():
                wq[slot, cc] = hq[q, cc]
                ws[slot, cc] = hs[q, cc]

    for cc in range(per):
        for slot in range(turns):

            @pl.when(w_from(slot) != me_grid)
            def _():
                for copy in w_arrival(cc, slot):
                    copy.wait_recv()

            for i in range(owned):
                out[i * TB : (i + 1) * TB, (slot * per + cc) * TB : (slot * per + cc + 1) * TB] = (
                    decode(wq[slot, cc, i], ws[slot, cc, i : i + 1, :])
                )

    for cc in range(per):
        for j in range(grid_size):

            @pl.when(me_grid < j)
            def _():
                for copy in z_copy(cc, j, 0, False):
                    copy.wait_send()

            @pl.when(me_grid > j)
            def _():
                for copy in z_copy(cc, j, 1, False):
                    copy.wait_send()

        for d in range(1, basis_size):
            for copy in x_copy(cc, d):
                copy.wait_send()
        for q in range(turns):

            @pl.when(w_place(q)[0] != me_grid)
            def _():
                for copy in w_copy(cc, q):
                    copy.wait_send()


def collect(coded, scales, takes, grid_size, basis_size, owned, turns):
    per = CL // grid_size
    members = CL // owned
    vmem = pl.BlockSpec(memory_space=pltpu.VMEM)

    def both(*lead):
        return [
            pltpu.VMEM(lead + (TB, TB), jnp.int16),
            pltpu.VMEM(lead + (TB,), jnp.float32),
        ]

    return pl.pallas_call(
        functools.partial(collect_kernel, grid_size, basis_size, owned, turns),
        out_shape=jax.ShapeDtypeStruct((owned * TB, turns * per * TB), jnp.float32),
        in_specs=[vmem] * 3,
        out_specs=vmem,
        scratch_shapes=both(2, grid_size, per, CL)
        + both(2, grid_size, per, CL)
        + both(per, members, owned)
        + both(basis_size - 1, per, owned)
        + both(turns, per, owned)
        + both(turns, per, owned)
        + [
            pltpu.SemaphoreType.DMA((2, grid_size, per, 2)),
            pltpu.SemaphoreType.DMA((2, grid_size, per, 2)),
            pltpu.SemaphoreType.DMA((basis_size - 1, per, 2)),
            pltpu.SemaphoreType.DMA((basis_size - 1, per, 2)),
            pltpu.SemaphoreType.DMA((turns, per, 2)),
            pltpu.SemaphoreType.DMA((turns, per, 2)),
        ],
        compiler_params=pltpu.CompilerParams(
            collective_id=0, has_side_effects=True, vmem_limit_bytes=48 * 1024 * 1024
        ),
        name="collect",
    )(coded, scales, takes)


def body(
    basis_values,
    weights,
    points,
    block_lists,
    counts,
    density,
    centers,
    block_centers,
    block_exponents,
):
    basis_size = lax.axis_size("basis")
    grid_size = lax.axis_size("grid")
    me_basis = lax.axis_index("basis")
    me_grid = lax.axis_index("grid")
    block_count = block_exponents.shape[0]
    owned_blocks = block_count // basis_size
    turns = block_count // CL
    per = CL // grid_size
    batches, point_total = weights.shape
    lists = block_lists.shape[1]

    first = first_block_of(block_lists, block_count)
    firsts = lax.all_to_all(
        jnp.broadcast_to(first, (basis_size, 1)), "basis", split_axis=0, concat_axis=0, tiled=True
    )[:, 0]
    my_residues = me_grid * per + jnp.arange(per, dtype=jnp.int32)
    columns = block_with_residue(firsts[:, None], my_residues[None, :], block_count)

    members = block_with_residue(first, jnp.arange(CL, dtype=jnp.int32), block_count)
    slots = (me_basis - members // owned_blocks) % basis_size

    coup = region_coupling(members, centers)
    boys = boys_table(
        points.astype(jnp.float32), block_lists, block_centers, block_exponents
    ).reshape(batches, lists * lists, point_total)
    live_count = counts[0, 0]
    is_live = jnp.arange(batches, dtype=jnp.int32) < live_count
    scaled = jnp.where(is_live[:, None], weights, 0.0) / point_total
    weighted = (basis_values * scaled[:, :, None]).astype(jnp.bfloat16)

    packed = pack_density(columns, density)
    dens = fetch_density(slots, packed, grid_size, basis_size, owned_blocks)
    coded, scales = region_exchange(
        block_lists % CL, counts.reshape(1), basis_values, weighted, boys, dens, coup, grid_size
    )
    back = (me_basis - jnp.arange(basis_size, dtype=jnp.int32)) % basis_size
    begins = firsts[back]
    my_blocks = me_basis * owned_blocks + jnp.arange(owned_blocks, dtype=jnp.int32)
    inside = (my_blocks[None, :] - begins[:, None]) % block_count < CL
    turn_at = block_with_residue(begins[:, None], my_residues[None, :], block_count) // CL
    takes = (
        inside[:, None, :, None]
        & (turn_at[:, :, None, None] == jnp.arange(turns, dtype=jnp.int32)[None, None, None, :])
    )
    takes = jnp.broadcast_to(
        takes.astype(jnp.float32)[..., None], takes.shape + (TB,)
    )
    return collect(coded, scales, takes, grid_size, basis_size, owned_blocks, turns)


def solution(mesh):
    placed = (
        P(("grid", "basis"), None, None),
        P(("grid", "basis"), None),
        P(("grid", "basis"), None, None),
        P(("grid", "basis"), None),
        P("basis", "grid"),
        P("basis", None),
        P(),
        P(),
        P(),
    )
    return jax.shard_map(
        body, mesh=mesh, in_specs=placed, out_specs=P("basis", "grid"), check_vma=False
    )
```

```python
import functools
import math

import jax
import jax.numpy as jnp
from jax import lax
from jax.experimental import pallas as pl
from jax.experimental.pallas import tpu as pltpu
from jax.sharding import PartitionSpec as P

TB = 128
CL = 8


def boys_table(points_f, blocks, block_centers, block_exponents):
    centre = block_centers[:, blocks]
    middle = 0.5 * (centre[:, :, :, None] + centre[:, :, None, :])
    exponents = block_exponents[blocks]
    rate_pair = 0.5 * (exponents[:, :, None] + exponents[:, None, :])
    offset = points_f.transpose(1, 0, 2)[:, :, None, None, :] - middle[:, :, :, :, None]
    distance = jnp.sum(offset * offset, axis=0)
    tau_value = rate_pair[:, :, :, None] * distance + 0.05
    root_value = jnp.sqrt(tau_value)
    return 0.5 * math.sqrt(math.pi) * lax.erf(root_value) / root_value


def first_block_of(block_lists, block_count):
    present = jnp.any(
        block_lists.reshape(-1)[:, None] == jnp.arange(block_count, dtype=jnp.int32)[None, :],
        axis=0,
    )
    begins = present & jnp.logical_not(jnp.roll(present, 1))
    return jnp.sum(jnp.where(begins, jnp.arange(block_count, dtype=jnp.int32), 0))


def block_with_residue(first, residue, block_count):
    return (first + (residue - first) % CL) % block_count


def region_coupling(members, centers):
    functions = (members[:, None] * TB + jnp.arange(TB, dtype=jnp.int32)[None, :]).reshape(CL * TB)
    where_at = centers[:, functions].reshape(3, CL, TB)
    spread = where_at[:, :, None, :, None] - where_at[:, None, :, None, :]
    distance = jnp.sum(spread * spread, axis=0)
    sharpness = float(centers.shape[1]) ** (2.0 / 3.0)
    return jnp.exp(-sharpness * distance).astype(jnp.bfloat16)


def pack_kernel(column_ref, dens_ref, out_ref, sems):
    targets, per = out_ref.shape[:2]

    def copy(t, c):
        at = pl.multiple_of(column_ref[t, c] * TB, TB)
        return pltpu.make_async_copy(
            dens_ref.at[:, pl.ds(at, TB)], out_ref.at[t, c], sems.at[t, c]
        )

    for c in range(per):
        for t in range(targets):
            copy(t, c).start()
    for c in range(per):
        for t in range(targets):
            copy(t, c).wait()


def pack_density(columns, density):
    targets, per = columns.shape
    rows = density.shape[0]
    return pl.pallas_call(
        pack_kernel,
        in_specs=[
            pl.BlockSpec(memory_space=pltpu.SMEM),
            pl.BlockSpec(memory_space=pl.ANY),
        ],
        out_specs=pl.BlockSpec(memory_space=pltpu.VMEM),
        out_shape=jax.ShapeDtypeStruct((targets, per, rows, TB), jnp.bfloat16),
        scratch_shapes=[pltpu.SemaphoreType.DMA((targets, per))],
        name="pack_density",
    )(columns, density)


def fetch_kernel(grid_size, basis_size, owned, slot_ref, packed, out, *scratch):
    per = CL // grid_size
    landed = scratch[:per]
    x_send, x_recv, z_send, z_recv = scratch[per:]
    me_grid = lax.axis_index("grid")
    me_basis = lax.axis_index("basis")
    mesh_ids = pl.DeviceIdType.MESH

    barrier = pltpu.get_barrier_semaphore()
    for d in (1, grid_size - 1):
        pl.semaphore_signal(
            barrier,
            inc=1,
            device_id=(lax.rem(me_grid + d, grid_size), me_basis),
            device_id_type=mesh_ids,
        )
    for d in range(1, basis_size):
        pl.semaphore_signal(
            barrier,
            inc=1,
            device_id=(me_grid, lax.rem(me_basis + d, basis_size)),
            device_id_type=mesh_ids,
        )
    pl.semaphore_wait(barrier, basis_size + 1)

    def x_copy(cc, d):
        to = lax.rem(me_basis + d, basis_size)
        return pltpu.make_async_remote_copy(
            src_ref=packed.at[to, cc],
            dst_ref=landed[cc].at[d],
            send_sem=x_send.at[d - 1, cc],
            recv_sem=x_recv.at[d - 1, cc],
            device_id=(me_grid, to),
            device_id_type=mesh_ids,
        )

    def z_copy(cc, j, side):
        step = 1 if side == 0 else grid_size - 1
        return pltpu.make_async_remote_copy(
            src_ref=out.at[j, cc],
            dst_ref=out.at[j, cc],
            send_sem=z_send.at[j, cc, side],
            recv_sem=z_recv.at[j, cc],
            device_id=(lax.rem(me_grid + step, grid_size), me_basis),
            device_id_type=mesh_ids,
        )

    def own(cc):
        landed[cc][0] = packed[me_basis, cc]
        for d in range(1, basis_size):
            x_copy(cc, d).wait_recv()
        for r in range(CL):
            out[me_grid, cc, r] = landed[cc][
                slot_ref[r], (r % owned) * TB : (r % owned + 1) * TB, :
            ]

        @pl.when(me_grid < grid_size - 1)
        def _():
            z_copy(cc, me_grid, 0).start()

        @pl.when(me_grid > 0)
        def _():
            z_copy(cc, me_grid, 1).start()

    def relay(cc, h):
        @pl.when(me_grid >= h)
        def _():
            z_copy(cc, me_grid - h, 0).wait_recv()

            @pl.when(me_grid < grid_size - 1)
            def _():
                z_copy(cc, me_grid - h, 0).start()

        @pl.when(me_grid + h < grid_size)
        def _():
            z_copy(cc, me_grid + h, 1).wait_recv()

            @pl.when(me_grid > 0)
            def _():
                z_copy(cc, me_grid + h, 1).start()

    for cc in range(per):
        for d in range(1, basis_size):
            x_copy(cc, d).start()
    for cc in range(per):
        own(cc)
        if grid_size > 1:
            relay(cc, 1)
    for h in range(2, grid_size):
        for cc in range(per):
            relay(cc, h)

    for cc in range(per):
        for d in range(1, basis_size):
            x_copy(cc, d).wait_send()
        for h in range(grid_size):

            @pl.when((me_grid >= h) & (me_grid < grid_size - 1))
            def _():
                z_copy(cc, me_grid - h, 0).wait_send()

            @pl.when((me_grid + h < grid_size) & (me_grid > 0))
            def _():
                z_copy(cc, me_grid + h, 1).wait_send()


def fetch_density(slots, packed, grid_size, basis_size, owned):
    per = CL // grid_size
    vmem = pl.BlockSpec(memory_space=pltpu.VMEM)
    return pl.pallas_call(
        functools.partial(fetch_kernel, grid_size, basis_size, owned),
        out_shape=jax.ShapeDtypeStruct((grid_size, per, CL, TB, TB), jnp.bfloat16),
        in_specs=[pl.BlockSpec(memory_space=pltpu.SMEM), vmem],
        out_specs=vmem,
        scratch_shapes=[pltpu.VMEM((basis_size, owned * TB, TB), jnp.bfloat16)] * per
        + [
            pltpu.SemaphoreType.DMA((basis_size - 1, per)),
            pltpu.SemaphoreType.DMA((basis_size - 1, per)),
            pltpu.SemaphoreType.DMA((grid_size, per, 2)),
            pltpu.SemaphoreType.DMA((grid_size, per)),
        ],
        compiler_params=pltpu.CompilerParams(
            collective_id=1, has_side_effects=True, vmem_limit_bytes=32 * 1024 * 1024
        ),
        name="fetch_density",
    )(slots, packed)


def encode(tile):
    top = jnp.maximum(jnp.max(jnp.abs(tile), axis=0, keepdims=True), 1e-30)
    steps = jnp.round(tile * (32767.0 / top))
    return steps.astype(jnp.int32).astype(jnp.int16), top * (1.0 / 32767.0)


def decode(coded, scale):
    return coded.astype(jnp.int32).astype(jnp.float32) * scale


def batch_kernel(
    per, owned, place_ref, count_ref, values_ref, weighted_ref, boys_ref, dens_ref, coup_ref, out_ref, scale_ref, acc
):
    n = pl.program_id(0)
    lists = place_ref.shape[1]
    group = values_ref.shape[0]
    halves = math.gcd(owned, 2)
    width = owned // halves

    @pl.when(n == 0)
    def _():
        acc[...] = jnp.zeros_like(acc)

    def one(b):
        at = [place_ref[n * group + b, t] for t in range(lists)]
        dens = jnp.concatenate(
            [
                jnp.concatenate([dens_ref[c // per, c % per, r] for c in at], axis=1)
                for r in at
            ],
            axis=0,
        )
        mapped = lax.dot_general(
            dens, values_ref[b], (((1,), (1,)), ((), ())), preferred_element_type=jnp.float32
        ).astype(jnp.bfloat16)
        total = None
        for u in range(lists):
            coup = jnp.concatenate([coup_ref[r, at[u]] for r in at], axis=0)
            part = jnp.dot(
                coup, mapped[u * TB : (u + 1) * TB], preferred_element_type=jnp.float32
            )
            part = jnp.concatenate(
                [
                    part[t * TB : (t + 1) * TB]
                    * boys_ref[b, t * lists + u : t * lists + u + 1, :]
                    for t in range(lists)
                ],
                axis=0,
            )
            total = part if total is None else total + part
        tile = jnp.dot(
            total.astype(jnp.bfloat16), weighted_ref[b], preferred_element_type=jnp.float32
        )
        return at, tile

    @pl.when(n * group < count_ref[0])
    def _():
        for at, tile in [one(b) for b in range(group)]:
            for c in range(lists):
                for r in range(lists):
                    acc[at[c], at[r]] += tile[c * TB : (c + 1) * TB, r * TB : (r + 1) * TB]

    @pl.when(n == pl.num_programs(0) - 1)
    def _():
        def put(index, carry):
            c = index // CL
            r = index % CL
            coded, scale = encode(acc[c, r].T)
            part = r % owned // width
            unit = c % per * halves + part
            row = r // owned * width + r % width
            out_ref[c // per, unit, row] = coded
            scale_ref[c // per, unit, pl.ds(row, 1), :] = scale
            return carry

        lax.fori_loop(0, CL * CL, put, 0)


def region_exchange(places, count, values, weighted, boys, dens, coup, grid_size, owned):
    batches, points, listed = values.shape
    per = CL // grid_size
    lists = places.shape[1]
    group = math.gcd(batches, 2)
    halves = math.gcd(owned, 2)
    units, rows = per * halves, CL // halves
    whole = lambda *shape: pl.BlockSpec(shape, lambda n, *_: (0,) * len(shape))
    return pl.pallas_call(
        functools.partial(batch_kernel, per, owned),
        grid_spec=pltpu.PrefetchScalarGridSpec(
            num_scalar_prefetch=2,
            grid=(batches // group,),
            in_specs=[
                pl.BlockSpec((group, points, listed), lambda n, *_: (n, 0, 0)),
                pl.BlockSpec((group, points, listed), lambda n, *_: (n, 0, 0)),
                pl.BlockSpec((group, lists * lists, points), lambda n, *_: (n, 0, 0)),
                whole(grid_size, per, CL, TB, TB),
                whole(CL, CL, TB, TB),
            ],
            out_specs=[
                whole(grid_size, units, rows, TB, TB),
                whole(grid_size, units, rows, TB),
            ],
            scratch_shapes=[pltpu.VMEM((CL, CL, TB, TB), jnp.float32)],
        ),
        out_shape=[
            jax.ShapeDtypeStruct((grid_size, units, rows, TB, TB), jnp.int16),
            jax.ShapeDtypeStruct((grid_size, units, rows, TB), jnp.float32),
        ],
        compiler_params=pltpu.CompilerParams(vmem_limit_bytes=48 * 1024 * 1024),
        name="region_exchange",
    )(places, count, values, weighted, boys, dens, coup)


def collect_kernel(
    grid_size,
    basis_size,
    owned,
    turns,
    kq,
    ks,
    takes,
    out,
    zq,
    zs,
    sq,
    ss,
    xq,
    xs,
    hq,
    hs,
    wq,
    ws,
    z_send,
    z_recv,
    x_send,
    x_recv,
    w_send,
    w_recv,
):
    per = CL // grid_size
    members = CL // owned
    per_owner = turns * per
    halves = math.gcd(owned, 2)
    width = owned // halves
    units = per * halves
    me_grid = lax.axis_index("grid")
    me_basis = lax.axis_index("basis")
    mine = lax.rem(me_basis, members)

    barrier = pltpu.get_barrier_semaphore()
    for d in range(1, grid_size):
        pl.semaphore_signal(
            barrier,
            inc=1,
            device_id=(lax.rem(me_grid + d, grid_size), me_basis),
            device_id_type=pl.DeviceIdType.MESH,
        )
    for d in range(1, basis_size):
        pl.semaphore_signal(
            barrier,
            inc=1,
            device_id=(me_grid, lax.rem(me_basis + d, basis_size)),
            device_id_type=pl.DeviceIdType.MESH,
        )
    pl.semaphore_wait(barrier, grid_size + basis_size - 2)

    def pair(sources, targets, sends, recvs, device):
        return [
            pltpu.make_async_remote_copy(
                src_ref=sources[which],
                dst_ref=targets[which],
                send_sem=sends.at[which],
                recv_sem=recvs.at[which],
                device_id=device,
                device_id_type=pl.DeviceIdType.MESH,
            )
            for which in range(2)
        ]

    def z_copy(cc, d):
        to = lax.rem(me_grid + d, grid_size)
        return pair(
            (kq.at[to, cc], ks.at[to, cc]),
            (zq.at[d - 1, cc], zs.at[d - 1, cc]),
            z_send.at[d - 1, cc],
            z_recv.at[d - 1, cc],
            (to, me_basis),
        )

    def x_copy(cc, d):
        to = lax.rem(me_basis + d, basis_size)
        its = lax.rem(to, members)
        return pair(
            (sq.at[cc, its], ss.at[cc, its]),
            (xq.at[d - 1, cc], xs.at[d - 1, cc]),
            x_send.at[d - 1, cc],
            x_recv.at[d - 1, cc],
            (me_grid, to),
        )

    def w_place(q):
        at = CL * q + me_grid * per
        return at // per_owner, lax.rem(at, per_owner) // per

    def w_copy(cc, q):
        to, slot = w_place(q)
        return pair(
            (hq.at[q, cc], hs.at[q, cc]),
            (wq.at[slot, cc], ws.at[slot, cc]),
            w_send.at[q, cc],
            w_recv.at[slot, cc],
            (to, me_basis),
        )

    def w_arrival(cc, slot):
        return pair(
            (hq.at[slot, cc], hs.at[slot, cc]),
            (wq.at[slot, cc], ws.at[slot, cc]),
            w_send.at[slot, cc],
            w_recv.at[slot, cc],
            (lax.rem(me_grid + 1, grid_size), me_basis),
        )

    def w_from(slot):
        return lax.rem(me_grid * per_owner + slot * per, CL) // per

    for cc in range(units):
        for d in range(1, grid_size):
            for copy in z_copy(cc, d):
                copy.start()

    for cc in range(units):
        for d in range(1, grid_size):
            for copy in z_copy(cc, d):
                copy.wait_recv()
        for m in range(members):

            def add_up(i, carry):
                r = m * width + i
                total = decode(kq[me_grid, cc, r], ks[me_grid, cc, pl.ds(r, 1), :])
                for d in range(1, grid_size):
                    total += decode(zq[d - 1, cc, r], zs[d - 1, cc, pl.ds(r, 1), :])
                sq[cc, m, i], ss[cc, m, pl.ds(i, 1), :] = encode(total)
                return carry

            lax.fori_loop(0, width, add_up, 0)
        for d in range(1, basis_size):
            for copy in x_copy(cc, d):
                copy.start()

    for cc in range(units):
        for d in range(1, basis_size):
            for copy in x_copy(cc, d):
                copy.wait_recv()
        for q in range(turns):

            def place(i, carry):
                total = decode(
                    sq[cc, mine, i], ss[cc, mine, pl.ds(i, 1), :] * takes[0, cc // halves, cc % halves * width + i, q : q + 1, :]
                )
                for d in range(1, basis_size):
                    total += decode(
                        xq[d - 1, cc, i],
                        xs[d - 1, cc, pl.ds(i, 1), :] * takes[d, cc // halves, cc % halves * width + i, q : q + 1, :],
                    )
                hq[q, cc, i], hs[q, cc, pl.ds(i, 1), :] = encode(total)
                return carry

            lax.fori_loop(0, width, place, 0)
            to, slot = w_place(q)

            @pl.when(to != me_grid)
            def _():
                for copy in w_copy(cc, q):
                    copy.start()

            @pl.when(to == me_grid)
            def _():
                wq[slot, cc] = hq[q, cc]
                ws[slot, cc] = hs[q, cc]

    for cc in range(units):
        for slot in range(turns):

            @pl.when(w_from(slot) != me_grid)
            def _():
                for copy in w_arrival(cc, slot):
                    copy.wait_recv()

            column = (slot * per + cc // halves) * TB
            for i in range(width):
                row = (cc % halves * width + i) * TB
                out[row : row + TB, column : column + TB] = decode(
                    wq[slot, cc, i], ws[slot, cc, i : i + 1, :]
                )

    for cc in range(units):
        for d in range(1, grid_size):
            for copy in z_copy(cc, d):
                copy.wait_send()
        for d in range(1, basis_size):
            for copy in x_copy(cc, d):
                copy.wait_send()
        for q in range(turns):

            @pl.when(w_place(q)[0] != me_grid)
            def _():
                for copy in w_copy(cc, q):
                    copy.wait_send()


def collect(coded, scales, takes, grid_size, basis_size, owned, turns):
    per = CL // grid_size
    members = CL // owned
    halves = math.gcd(owned, 2)
    width = owned // halves
    units = per * halves
    vmem = pl.BlockSpec(memory_space=pltpu.VMEM)

    def both(*lead):
        return [
            pltpu.VMEM(lead + (TB, TB), jnp.int16),
            pltpu.VMEM(lead + (TB,), jnp.float32),
        ]

    return pl.pallas_call(
        functools.partial(collect_kernel, grid_size, basis_size, owned, turns),
        out_shape=jax.ShapeDtypeStruct((owned * TB, turns * per * TB), jnp.float32),
        in_specs=[vmem] * 3,
        out_specs=vmem,
        scratch_shapes=both(grid_size - 1, units, members * width)
        + both(units, members, width)
        + both(basis_size - 1, units, width)
        + both(turns, units, width)
        + both(turns, units, width)
        + [
            pltpu.SemaphoreType.DMA((grid_size - 1, units, 2)),
            pltpu.SemaphoreType.DMA((grid_size - 1, units, 2)),
            pltpu.SemaphoreType.DMA((basis_size - 1, units, 2)),
            pltpu.SemaphoreType.DMA((basis_size - 1, units, 2)),
            pltpu.SemaphoreType.DMA((turns, units, 2)),
            pltpu.SemaphoreType.DMA((turns, units, 2)),
        ],
        compiler_params=pltpu.CompilerParams(
            collective_id=0, has_side_effects=True, vmem_limit_bytes=48 * 1024 * 1024
        ),
        name="collect",
    )(coded, scales, takes)


def body(
    basis_values,
    weights,
    points,
    block_lists,
    counts,
    density,
    centers,
    block_centers,
    block_exponents,
):
    basis_size = lax.axis_size("basis")
    grid_size = lax.axis_size("grid")
    me_basis = lax.axis_index("basis")
    me_grid = lax.axis_index("grid")
    block_count = block_exponents.shape[0]
    owned_blocks = block_count // basis_size
    turns = block_count // CL
    per = CL // grid_size
    batches, point_total = weights.shape
    lists = block_lists.shape[1]

    first = first_block_of(block_lists, block_count)
    firsts = lax.all_to_all(
        jnp.broadcast_to(first, (basis_size, 1)), "basis", split_axis=0, concat_axis=0, tiled=True
    )[:, 0]
    my_residues = me_grid * per + jnp.arange(per, dtype=jnp.int32)
    columns = block_with_residue(firsts[:, None], my_residues[None, :], block_count)

    members = block_with_residue(first, jnp.arange(CL, dtype=jnp.int32), block_count)
    slots = (me_basis - members // owned_blocks) % basis_size

    coup = region_coupling(members, centers)
    boys = boys_table(
        points.astype(jnp.float32), block_lists, block_centers, block_exponents
    ).reshape(batches, lists * lists, point_total)
    live_count = counts[0, 0]
    is_live = jnp.arange(batches, dtype=jnp.int32) < live_count
    scaled = jnp.where(is_live[:, None], weights, 0.0) / point_total
    weighted = (basis_values * scaled[:, :, None]).astype(jnp.bfloat16)

    packed = pack_density(columns, density)
    dens = fetch_density(slots, packed, grid_size, basis_size, owned_blocks)
    coded, scales = region_exchange(
        block_lists % CL, counts.reshape(1), basis_values, weighted, boys, dens, coup, grid_size,
        owned_blocks,
    )
    back = (me_basis - jnp.arange(basis_size, dtype=jnp.int32)) % basis_size
    begins = firsts[back]
    my_blocks = me_basis * owned_blocks + jnp.arange(owned_blocks, dtype=jnp.int32)
    inside = (my_blocks[None, :] - begins[:, None]) % block_count < CL
    turn_at = block_with_residue(begins[:, None], my_residues[None, :], block_count) // CL
    takes = (
        inside[:, None, :, None]
        & (turn_at[:, :, None, None] == jnp.arange(turns, dtype=jnp.int32)[None, None, None, :])
    )
    takes = jnp.broadcast_to(
        takes.astype(jnp.float32)[..., None], takes.shape + (TB,)
    )
    return collect(coded, scales, takes, grid_size, basis_size, owned_blocks, turns)


def solution(mesh):
    placed = (
        P(("grid", "basis"), None, None),
        P(("grid", "basis"), None),
        P(("grid", "basis"), None, None),
        P(("grid", "basis"), None),
        P("basis", "grid"),
        P("basis", None),
        P(),
        P(),
        P(),
    )
    return jax.shard_map(
        body, mesh=mesh, in_specs=placed, out_specs=P("basis", "grid"), check_vma=False
    )
```
